32 devices in a mesh: ctx: 16 (over z, x, core), head: 2 (over y).
Axes of the slice: x: 2, y: 2, z: 4, core: 2. Of those that a mesh axis runs over, the one named last changes fastest.
Arguments:
- queries: bfloat16 [2048, 64, 576], P('ctx', 'head'), may hold values from -512 to 512
- latents: bfloat16 [2048, 576], P('ctx'), may hold values from -4 to 4
- index_queries: bfloat16 [2048, 64, 128], P('ctx', 'head'), may hold values from -512 to 512
- index_keys: bfloat16 [2048, 128], P('ctx'), may hold values from -4 to 4
- head_weights: float32 [2048, 64], P('ctx', 'head'), may hold values from -1.5 to 1.5
- block_pos: int32 [16], replicated, may hold values from 0 to 15, each once
Outputs:
- grad_index_queries: float32 [2048, 64, 128], P('ctx', 'head')
- grad_index_keys: float32 [2048, 128], P('ctx')
The draws below stay inside these ranges and needn't reach their ends.
All inputs are finite; a program needn't handle non-finite values.
Results may differ from the reference program's by a relative error of at most 0.008.
Values may be sent and summed in bfloat16 or wider, within the bound.
A program may use at most 128 MiB of HBM per device.

```python
import jax
import jax.numpy as jnp
from jax import lax

HEADS = 64
RANK = 576
IHEADS = 64
IDIM = 128
TOK_DEV = 128
SEQ = 2048
BLOCKS = 16


def context_draw(key):
    pieces = jax.random.split(jax.random.fold_in(key, 7), 5)
    latent = jnp.clip(jax.random.normal(pieces[0], (SEQ, RANK), jnp.float32), -4.0, 4.0)
    latent = latent.astype(jnp.bfloat16).astype(jnp.float32)
    ikeys = jnp.clip(jax.random.normal(pieces[1], (SEQ, IDIM), jnp.float32), -4.0, 4.0)
    ikeys = ikeys.astype(jnp.bfloat16).astype(jnp.float32)
    weights = jnp.clip(0.3 * jax.random.normal(pieces[2], (SEQ, IHEADS), jnp.float32), -1.5, 1.5)
    query = jnp.clip(jax.random.normal(pieces[3], (SEQ, HEADS, RANK), jnp.float32), -4.0, 4.0)
    iquery = jnp.clip(jax.random.normal(pieces[4], (SEQ, IHEADS, IDIM), jnp.float32), -4.0, 4.0)
    return (latent, ikeys, weights, query, iquery)


def draw_latents(key, part):
    return context_draw(key)[0].astype(jnp.bfloat16)


def draw_index_keys(key, part):
    return context_draw(key)[1].astype(jnp.bfloat16)


def draw_head_weights(key, part):
    return context_draw(key)[2]


def draw_queries(key, part):
    return context_draw(key)[3].astype(jnp.bfloat16)


def draw_index_queries(key, part):
    return context_draw(key)[4].astype(jnp.bfloat16)


def setup_inputs(seed: int = 0) -> dict:
    seeds = jax.random.split(jax.random.key(seed), 7)
    return {
        "queries": draw_queries(jax.random.fold_in(seeds[6], 71), 0),
        "latents": draw_latents(jax.random.fold_in(seeds[6], 71), 0),
        "index_queries": draw_index_queries(jax.random.fold_in(seeds[6], 71), 0),
        "index_keys": draw_index_keys(jax.random.fold_in(seeds[6], 71), 0),
        "head_weights": draw_head_weights(jax.random.fold_in(seeds[6], 71), 0),
        "block_pos": jax.random.permutation(seeds[5], BLOCKS).astype(jnp.int32),
    }


SCALE_ATTN = 192.0 ** -0.5
LOSS_SCALE = 1024.0
NEGATIVE = -1.0e30


def positions(block_pos):
    stored = jnp.arange(SEQ, dtype=jnp.int32)
    return block_pos[stored // TOK_DEV] * TOK_DEV + stored % TOK_DEV


def reference(queries, latents, index_queries, index_keys, head_weights, block_pos):
    place = positions(block_pos)
    visible = place[None, :] <= place[:, None]
    index_scale = IDIM ** -0.5
    latent_wide = latents.astype(jnp.float32)
    keys_wide = index_keys.astype(jnp.float32)

    def attend(summed, query_head):
        scores = SCALE_ATTN * jnp.dot(query_head.astype(jnp.float32), latent_wide.T, precision=lax.Precision.HIGHEST)
        scores = jnp.where(visible, scores, NEGATIVE)
        row_top = jnp.max(scores, axis=1, keepdims=True)
        weights = jnp.where(visible, jnp.exp(scores - row_top), 0.0)
        return summed + weights / jnp.sum(weights, axis=1, keepdims=True), None

    target, _ = lax.scan(attend, jnp.zeros((SEQ, SEQ), jnp.float32), jnp.swapaxes(queries, 0, 1))
    target = target / HEADS

    def index_head(summed, inputs):
        query_head, weight = inputs
        dots = jnp.dot(query_head.astype(jnp.float32), keys_wide.T, precision=lax.Precision.HIGHEST)
        return summed + weight[:, None] * jnp.maximum(dots, 0.0) * index_scale, None

    stacked = (jnp.swapaxes(index_queries, 0, 1), head_weights.T)
    index, _ = lax.scan(index_head, jnp.zeros((SEQ, SEQ), jnp.float32), stacked)
    masked = jnp.where(visible, index, NEGATIVE)
    row_top = jnp.max(masked, axis=1, keepdims=True)
    weights = jnp.where(visible, jnp.exp(masked - row_top), 0.0)
    prob = weights / jnp.sum(weights, axis=1, keepdims=True)
    delta = jnp.where(visible, LOSS_SCALE * (prob - target), 0.0).astype(jnp.bfloat16)
    delta_wide = lax.optimization_barrier(delta).astype(jnp.float32)

    def backward(summed, inputs):
        query_head, weight = inputs
        query_wide = query_head.astype(jnp.float32)
        dots = jnp.dot(query_wide, keys_wide.T, precision=lax.Precision.HIGHEST)
        coef = jnp.where(dots > 0.0, delta_wide * weight[:, None] * index_scale, 0.0).astype(jnp.bfloat16)
        coef = lax.optimization_barrier(coef).astype(jnp.float32)
        grad_query = jnp.dot(coef, keys_wide, precision=lax.Precision.HIGHEST)
        return summed + jnp.dot(coef.T, query_wide, precision=lax.Precision.HIGHEST), grad_query

    grad_keys, grad_queries = lax.scan(backward, jnp.zeros((SEQ, IDIM), jnp.float32), stacked)
    return jnp.swapaxes(grad_queries, 0, 1), grad_keys
```

```python
import functools
import math

import jax
import jax.numpy as jnp
from jax import lax
from jax.experimental import pallas as pl
from jax.experimental.pallas import tpu as pltpu
from jax.sharding import PartitionSpec as P

HEADS = 64
SCALE_ATTN = 192.0 ** (-0.5)
LOSS_SCALE = 1024.0
NEGATIVE = -1e30
LOG2E = math.log2(math.e)
MESH = pl.DeviceIdType.MESH
F32 = jnp.float32
BF16 = jnp.bfloat16
TOK = 8
VMEM_LIMIT = 60 * 1024 * 1024


def place(n):
    me = lax.axis_index("ctx")
    a = n // 4
    return me // 4, (me // 2) % 2, me % 2, a


def at(z, x, c):
    return (z * 2 + x) * 2 + c


def remote(src, dst, send, recv, **where):
    return pltpu.make_async_remote_copy(
        src_ref=src, dst_ref=dst, send_sem=send, recv_sem=recv, device_id=where, device_id_type=MESH
    )


def gather_kernel(n, lat_ref, key_ref, lat_out, key_out, send_sem, recv_sem, own_sem):
    z, x, c, a = place(n)
    up, down = z + 1 < a, z > 0
    barrier = pltpu.get_barrier_semaphore()

    def greet(index):
        pl.semaphore_signal(barrier, inc=1, device_id={"ctx": index}, device_id_type=MESH)

    greet(at(z, 1 - x, c))
    greet(at(z, x, 1 - c))

    @pl.when(up)
    def _():
        greet(at(z + 1, x, c))

    @pl.when(down)
    def _():
        greet(at(z - 1, x, c))

    me = at(z, x, c)
    owns = []
    for k, (src, dst) in enumerate(((key_ref, key_out), (lat_ref, lat_out))):
        own = pltpu.make_async_copy(src, dst.at[me], own_sem.at[k])
        own.start()
        owns.append(own)
    pl.semaphore_wait(barrier, 2 + up.astype(jnp.int32) + down.astype(jnp.int32))

    outs = (key_out, lat_out)
    ins = (key_ref, lat_ref)

    def copy(k, slot, way, target, first):
        src = ins[k] if first else outs[k].at[slot]
        return remote(
            src, outs[k].at[slot], send_sem.at[k, slot, way], recv_sem.at[k, slot], ctx=target
        )

    def arrived(k, slot):
        copy(k, slot, 0, at(z, x, 1 - c), False).wait_recv()

    def ways(k, zs, d, side, act):
        slot = at(zs, x, c)
        first = d == 0
        if side >= 0:

            @pl.when(up)
            def _():
                act(copy(k, slot, 2, at(z + 1, x, c), first))

        if side <= 0:

            @pl.when(down)
            def _():
                act(copy(k, slot, 3, at(z - 1, x, c), first))

        act(copy(k, slot, 1, at(z, 1 - x, c), first))
        act(copy(k, slot, 0, at(z, x, 1 - c), first))

    def each(d, side):
        zs = z - d if side >= 0 else z + d
        ok = zs >= 0 if side >= 0 else zs < a
        return zs, ok

    start = lambda item: item.start()
    done = lambda item: item.wait_send()
    for k in range(2):
        ways(k, z, 0, 0, start)
    for d in range(1, a):
        for k in range(2):
            for side in (1, -1):
                zs, ok = each(d, side)

                @pl.when(ok)
                def _():
                    arrived(k, at(zs, x, c))
                    ways(k, zs, d, side, start)

            for side in (1, -1) if d > 1 else (1,):
                zs, ok = each(d - 1, side)

                @pl.when(ok)
                def _():
                    slot = at(zs, 1 - x, c)
                    arrived(k, slot)
                    copy(k, slot, 0, at(z, x, 1 - c), False).start()

    for k in range(2):
        for side in (1, -1):
            zs, ok = each(a - 1, side)

            @pl.when(ok)
            def _():
                slot = at(zs, 1 - x, c)
                arrived(k, slot)
                copy(k, slot, 0, at(z, x, 1 - c), False).start()

    for k in range(2):
        owns[k].wait()
        for zs in range(a):
            for xs in range(2):
                arrived(k, at(zs, xs, 1 - c))
        ways(k, z, 0, 0, done)
        for d in range(1, a):
            for side in (1, -1):
                zs, ok = each(d, side)

                @pl.when(ok)
                def _():
                    ways(k, zs, d, side, done)

        for zs in range(a):
            copy(k, at(zs, 1 - x, c), 0, at(z, x, 1 - c), False).wait_send()


def gather(latents, keys, n):
    rows = latents.shape[0]
    hbm = pl.BlockSpec(memory_space=pl.ANY)
    return pl.pallas_call(
        functools.partial(gather_kernel, n),
        out_shape=(
            jax.ShapeDtypeStruct((n, rows, latents.shape[1]), BF16),
            jax.ShapeDtypeStruct((n, rows, keys.shape[1]), BF16),
        ),
        in_specs=[hbm, hbm],
        out_specs=(hbm, hbm),
        scratch_shapes=[
            pltpu.SemaphoreType.DMA((2, n, 4)),
            pltpu.SemaphoreType.DMA((2, n)),
            pltpu.SemaphoreType.DMA((2,)),
        ],
        compiler_params=pltpu.CompilerParams(collective_id=0, has_side_effects=True),
        name="gather",
    )(latents, keys)


def dot_t(a, b):
    return lax.dot_general(a, b, (((1,), (1,)), ((), ())), preferred_element_type=F32)


def index_kernel(heads, iq_ref, w_ref, key_ref, out_ref, scr):
    scr[...] = dot_t(iq_ref[...], key_ref[...])
    rows = []
    for t in range(TOK):
        acc = None
        for g in range(0, heads, 8):
            r = t * heads + g
            w = w_ref[r : r + 8, 0:1]
            part = jnp.maximum(scr[r : r + 8, :], 0.0) * w
            acc = part if acc is None else acc + part
        rows.append(jnp.sum(acc, axis=0, keepdims=True))
    out_ref[...] = jnp.concatenate(rows, axis=0)


def index_part(iq, wide, keys, heads):
    total, depth = iq.shape
    seq = keys.shape[0]
    m = TOK * heads
    return pl.pallas_call(
        functools.partial(index_kernel, heads),
        grid=(total // m,),
        out_shape=jax.ShapeDtypeStruct((total // heads, seq), F32),
        in_specs=[
            pl.BlockSpec((m, depth), lambda i: (i, 0)),
            pl.BlockSpec((m, wide.shape[1]), lambda i: (i, 0)),
            pl.BlockSpec((seq, depth), lambda i: (0, 0)),
        ],
        out_specs=pl.BlockSpec((TOK, seq), lambda i: (i, 0)),
        scratch_shapes=[pltpu.VMEM((m, seq), F32)],
        compiler_params=pltpu.CompilerParams(vmem_limit_bytes=VMEM_LIMIT),
        cost_estimate=pl.CostEstimate(
            flops=4 * total * seq * depth, bytes_accessed=4 * total * depth, transcendentals=0
        ),
        name="index_part",
    )(iq, wide, keys)


def attend_kernel(heads, q_ref, lat_ref, post_ref, poss_ref, out_ref, low_ref, scr, bias):
    scr[...] = dot_t(q_ref[...], lat_ref[...])
    bias[...] = jnp.where(poss_ref[...] <= post_ref[...], 0.0, NEGATIVE)
    rows = []
    for t in range(TOK):
        acc = None
        for g in range(0, heads, 8):
            r = t * heads + g
            s = scr[r : r + 8, :] + bias[t : t + 1, :]
            top = jnp.max(s, axis=1, keepdims=True)
            p = jnp.exp2((s - top) * (SCALE_ATTN * LOG2E))
            part = p * (1.0 / (HEADS * jnp.sum(p, axis=1, keepdims=True)))
            acc = part if acc is None else acc + part
        rows.append(jnp.sum(acc, axis=0, keepdims=True))
    out = jnp.concatenate(rows, axis=0)
    out_ref[...] = out
    low_ref[...] = out.astype(BF16)


def attend(q, lat, pos_t, pos_s, heads, first, count):
    depth = q.shape[1]
    seq = lat.shape[0]
    m = TOK * heads
    off = first // TOK
    return pl.pallas_call(
        functools.partial(attend_kernel, heads),
        grid=(count // TOK,),
        out_shape=(
            jax.ShapeDtypeStruct((count, seq), F32),
            jax.ShapeDtypeStruct((count, seq), BF16),
        ),
        in_specs=[
            pl.BlockSpec((m, depth), lambda i: (i + off, 0)),
            pl.BlockSpec((seq, depth), lambda i: (0, 0)),
            pl.BlockSpec((TOK, 1), lambda i: (i + off, 0)),
            pl.BlockSpec((1, seq), lambda i: (0, 0)),
        ],
        out_specs=(
            pl.BlockSpec((TOK, seq), lambda i: (i, 0)),
            pl.BlockSpec((TOK, seq), lambda i: (i, 0)),
        ),
        scratch_shapes=[pltpu.VMEM((m, seq), F32), pltpu.VMEM((TOK, seq), F32)],
        compiler_params=pltpu.CompilerParams(vmem_limit_bytes=VMEM_LIMIT),
        cost_estimate=pl.CostEstimate(
            flops=4 * count * heads * seq * depth,
            bytes_accessed=2 * count * heads * depth,
            transcendentals=count * heads * seq,
        ),
        name="attend",
    )(q, lat, pos_t, pos_s)


def back_kernel(heads, last, iq_ref, w_ref, key_ref, post_ref, poss_ref, *rest):
    peers_i = rest[0]
    own_i, own_t, peers_t, carry, gq_ref, gk_ref, scr, coef, acc, dscr = rest[1:]
    step = pl.program_id(0)

    @pl.when(step == 0)
    def _():
        acc[...] = carry[...]

    scr[...] = dot_t(iq_ref[...], key_ref[...])
    index, target = own_i[...], own_t[...]
    for k in range(peers_i.shape[0]):
        index = index + peers_i[k]
        target = target + peers_t[k].astype(F32)
    seen = poss_ref[...] <= post_ref[...]
    masked = jnp.where(seen, index, NEGATIVE)
    weights = jnp.where(seen, jnp.exp(masked - jnp.max(masked, axis=1, keepdims=True)), 0.0)
    prob = weights * (1.0 / jnp.sum(weights, axis=1, keepdims=True))
    dscr[...] = jnp.where(seen, LOSS_SCALE * (prob - target), 0.0).astype(BF16).astype(F32)
    for t in range(TOK):
        for g in range(0, heads, 8):
            r = t * heads + g
            value = dscr[t : t + 1, :] * w_ref[r : r + 8, 0:1]
            coef[r : r + 8, :] = jnp.where(scr[r : r + 8, :] > 0.0, value, 0.0).astype(BF16)
    gq_ref[...] = jnp.dot(coef[...], key_ref[...], preferred_element_type=F32)
    acc[...] += lax.dot_general(
        iq_ref[...], coef[...], (((0,), (0,)), ((), ())), preferred_element_type=F32
    )

    @pl.when(step == pl.num_programs(0) - 1)
    def _():
        if last:
            gk_ref[...] = jnp.transpose(acc[...]).astype(BF16)
        else:
            gk_ref[...] = acc[...]


def back(iq, wide, keys, pos_t, pos_s, peers_i, own_i, own_t, peers_t, carry, heads, first, last):
    depth = iq.shape[1]
    seq = keys.shape[0]
    count = own_t.shape[0]
    m = TOK * heads
    off = first // TOK
    others = peers_i.shape[0]
    return pl.pallas_call(
        functools.partial(back_kernel, heads, last),
        grid=(count // TOK,),
        out_shape=(
            jax.ShapeDtypeStruct((count * heads, depth), F32),
            jax.ShapeDtypeStruct((seq, depth), BF16)
            if last
            else jax.ShapeDtypeStruct((depth, seq), F32),
        ),
        in_specs=[
            pl.BlockSpec((m, depth), lambda i: (i + off, 0)),
            pl.BlockSpec((m, wide.shape[1]), lambda i: (i + off, 0)),
            pl.BlockSpec((seq, depth), lambda i: (0, 0)),
            pl.BlockSpec((TOK, 1), lambda i: (i + off, 0)),
            pl.BlockSpec((1, seq), lambda i: (0, 0)),
            pl.BlockSpec((others, TOK, seq), lambda i: (0, i + off, 0)),
            pl.BlockSpec((TOK, seq), lambda i: (i + off, 0)),
            pl.BlockSpec((TOK, seq), lambda i: (i, 0)),
            pl.BlockSpec((others, TOK, seq), lambda i: (0, i, 0)),
            pl.BlockSpec((depth, seq), lambda i: (0, 0)),
        ],
        out_specs=(
            pl.BlockSpec((m, depth), lambda i: (i, 0)),
            pl.BlockSpec((seq, depth) if last else (depth, seq), lambda i: (0, 0)),
        ),
        scratch_shapes=[
            pltpu.VMEM((m, seq), F32),
            pltpu.VMEM((m, seq), BF16),
            pltpu.VMEM((depth, seq), F32),
            pltpu.VMEM((TOK, seq), F32),
        ],
        compiler_params=pltpu.CompilerParams(vmem_limit_bytes=VMEM_LIMIT),
        cost_estimate=pl.CostEstimate(
            flops=8 * count * heads * seq * depth,
            bytes_accessed=8 * count * heads * depth,
            transcendentals=0,
        ),
        name="back",
    )(iq, wide, keys, pos_t, pos_s, peers_i, own_i, own_t, peers_t, carry)


def scatter_kernel(
    n, ranks, gk_ref, out_ref, got1, sum1, put2, got2, sum2, put3, got3, put4, got4, ssem, rsem
):
    z, x, c, a = place(n)
    y = lax.axis_index("head")
    barrier = pltpu.get_barrier_semaphore()
    greeted = [dict(ctx=at(z, 1 - x, c)), dict(ctx=at(z, x, 1 - c))]
    greeted += [dict(ctx=at(lax.rem(z + d, a), x, c)) for d in range(1, a)]
    greeted += [dict(head=lax.rem(y + d, ranks)) for d in range(1, ranks)]
    for where in greeted:
        pl.semaphore_signal(barrier, inc=1, device_id=where, device_id_type=MESH)
    pl.semaphore_wait(barrier, len(greeted))

    first = remote(gk_ref.at[:, :, 1 - c], got1, ssem.at[0], rsem.at[0], ctx=at(z, x, 1 - c))
    first.start()
    first.wait()
    sum1[...] = gk_ref[:, :, c].astype(F32) + got1[...].astype(F32)
    put2[...] = sum1[:, 1 - x].astype(BF16)
    second = remote(put2, got2, ssem.at[1], rsem.at[1], ctx=at(z, 1 - x, c))
    second.start()
    second.wait()
    sum2[...] = sum1[:, x] + got2[...].astype(F32)
    put3[...] = sum2[...].astype(BF16)
    third = []
    for d in range(1, a):
        to = lax.rem(z + d, a)
        item = remote(
            put3.at[to], got3.at[d - 1], ssem.at[1 + d], rsem.at[1 + d], ctx=at(to, x, c)
        )
        item.start()
        third.append(item)
    for item in third:
        item.wait()
    part = sum2[z]
    for d in range(1, a):
        part = part + got3[d - 1].astype(F32)
    put4[...] = part
    fourth = []
    for d in range(1, ranks):
        item = remote(
            put4,
            got4.at[d - 1],
            ssem.at[a + d],
            rsem.at[a + d],
            head=lax.rem(y + d, ranks),
        )
        item.start()
        fourth.append(item)
    for item in fourth:
        item.wait()
    part = put4[...]
    for d in range(1, ranks):
        part = part + got4[d - 1]
    out_ref[...] = part


def scatter(gk, n, ranks):
    a = n // 4
    rows, depth = gk.shape[0] // n, gk.shape[1]
    vmem = pl.BlockSpec(memory_space=pltpu.VMEM)
    return pl.pallas_call(
        functools.partial(scatter_kernel, n, ranks),
        out_shape=jax.ShapeDtypeStruct((rows, depth), F32),
        in_specs=[vmem],
        out_specs=vmem,
        scratch_shapes=[
            pltpu.VMEM((a, 2, rows, depth), BF16),
            pltpu.VMEM((a, 2, rows, depth), F32),
            pltpu.VMEM((a, rows, depth), BF16),
            pltpu.VMEM((a, rows, depth), BF16),
            pltpu.VMEM((a, rows, depth), F32),
            pltpu.VMEM((a, rows, depth), BF16),
            pltpu.VMEM((a - 1, rows, depth), BF16),
            pltpu.VMEM((rows, depth), F32),
            pltpu.VMEM((ranks - 1, rows, depth), F32),
            pltpu.SemaphoreType.DMA((a + ranks,)),
            pltpu.SemaphoreType.DMA((a + ranks,)),
        ],
        compiler_params=pltpu.CompilerParams(collective_id=1, has_side_effects=True),
        name="scatter",
    )(gk.reshape(a, 2, 2, rows, depth))


def swap(value, ranks):
    return jnp.stack(
        [
            lax.ppermute(value, "head", [(i, (i + d) % ranks) for i in range(ranks)])
            for d in range(1, ranks)
        ]
    )


def body(queries, latents, index_queries, index_keys, head_weights, block_pos):
    rows, heads, rank = queries.shape
    depth = index_queries.shape[2]
    n, ranks = lax.axis_size("ctx"), lax.axis_size("head")
    seq = rows * n
    q = queries.reshape(rows * heads, rank)
    iq = index_queries.reshape(rows * heads, depth)
    wide = jnp.broadcast_to(
        (head_weights * depth ** (-0.5))[:, :, None], (rows, heads, 128)
    ).reshape(rows * heads, 128)
    local = jnp.arange(rows, dtype=jnp.int32)
    pos_s = (block_pos[:, None] * rows + local[None, :]).reshape(1, seq)
    mine = jnp.sum(jnp.where(jnp.arange(n) == lax.axis_index("ctx"), block_pos, 0))
    pos_t = (mine * rows + local)[:, None]

    lat, keys = gather(latents, index_keys, n)
    lat = lat.reshape(seq, rank)
    keys = keys.reshape(seq, depth)
    own_i = index_part(iq, wide, keys, heads)
    peers_i = swap(own_i, ranks)
    half = rows // 2
    own_t, peers_t = [], []
    for k in range(2):
        full, low = attend(q, lat, pos_t, pos_s, heads, k * half, half)
        own_t.append(full)
        peers_t.append(swap(low, ranks))
    carry = jnp.zeros((depth, seq), F32)
    grads = []
    for k in range(2):
        gq, carry = back(
            iq, wide, keys, pos_t, pos_s, peers_i, own_i, own_t[k], peers_t[k], carry, heads,
            k * half, k == 1,
        )
        grads.append(gq)
    grad_queries = jnp.concatenate(grads, 0).reshape(rows, heads, depth)
    return grad_queries, scatter(carry, n, ranks)


def solution(mesh):
    return jax.shard_map(
        body,
        mesh=mesh,
        in_specs=(
            P("ctx", "head", None),
            P("ctx", None),
            P("ctx", "head", None),
            P("ctx", None),
            P("ctx", "head"),
            P(),
        ),
        out_specs=(P("ctx", "head", None), P("ctx", None)),
        check_vma=False,
    )
```

```python
import functools
import math

import jax
import jax.numpy as jnp
from jax import lax
from jax.experimental import pallas as pl
from jax.experimental.pallas import tpu as pltpu
from jax.sharding import PartitionSpec as P

HEADS = 64
SCALE_ATTN = 192.0 ** (-0.5)
LOSS_SCALE = 1024.0
NEGATIVE = -1e30
LOG2E = math.log2(math.e)
MESH = pl.DeviceIdType.MESH
F32 = jnp.float32
BF16 = jnp.bfloat16
TOK = 8
VMEM_LIMIT = 60 * 1024 * 1024


def place(n):
    me = lax.axis_index("ctx")
    a = n // 4
    return me // 4, (me // 2) % 2, me % 2, a


def at(z, x, c):
    return (z * 2 + x) * 2 + c


def remote(src, dst, send, recv, **where):
    return pltpu.make_async_remote_copy(
        src_ref=src, dst_ref=dst, send_sem=send, recv_sem=recv, device_id=where, device_id_type=MESH
    )


def gather_kernel(n, lat_ref, key_ref, lat_out, key_out, send_sem, recv_sem, own_sem):
    z, x, c, a = place(n)
    up, down = z + 1 < a, z > 0
    barrier = pltpu.get_barrier_semaphore()

    def greet(index):
        pl.semaphore_signal(barrier, inc=1, device_id={"ctx": index}, device_id_type=MESH)

    greet(at(z, 1 - x, c))
    greet(at(z, x, 1 - c))

    @pl.when(up)
    def _():
        greet(at(z + 1, x, c))

    @pl.when(down)
    def _():
        greet(at(z - 1, x, c))

    me = at(z, x, c)
    owns = []
    for k, (src, dst) in enumerate(((key_ref, key_out), (lat_ref, lat_out))):
        own = pltpu.make_async_copy(src, dst.at[me], own_sem.at[k])
        own.start()
        owns.append(own)
    pl.semaphore_wait(barrier, 2 + up.astype(jnp.int32) + down.astype(jnp.int32))

    outs = (key_out, lat_out)
    ins = (key_ref, lat_ref)

    def copy(k, slot, way, target, first):
        src = ins[k] if first else outs[k].at[slot]
        return remote(
            src, outs[k].at[slot], send_sem.at[k, slot, way], recv_sem.at[k, slot], ctx=target
        )

    def arrived(k, slot):
        copy(k, slot, 0, at(z, x, 1 - c), False).wait_recv()

    def ways(k, zs, d, side, act):
        slot = at(zs, x, c)
        first = d == 0
        if side >= 0:

            @pl.when(up)
            def _():
                act(copy(k, slot, 2, at(z + 1, x, c), first))

        if side <= 0:

            @pl.when(down)
            def _():
                act(copy(k, slot, 3, at(z - 1, x, c), first))

        act(copy(k, slot, 1, at(z, 1 - x, c), first))
        act(copy(k, slot, 0, at(z, x, 1 - c), first))

    def each(d, side):
        zs = z - d if side >= 0 else z + d
        ok = zs >= 0 if side >= 0 else zs < a
        return zs, ok

    start = lambda item: item.start()
    done = lambda item: item.wait_send()
    for k in range(2):
        ways(k, z, 0, 0, start)
    for d in range(1, a):
        for k in range(2):
            for side in (1, -1):
                zs, ok = each(d, side)

                @pl.when(ok)
                def _():
                    arrived(k, at(zs, x, c))
                    ways(k, zs, d, side, start)

            for side in (1, -1) if d > 1 else (1,):
                zs, ok = each(d - 1, side)

                @pl.when(ok)
                def _():
                    slot = at(zs, 1 - x, c)
                    arrived(k, slot)
                    copy(k, slot, 0, at(z, x, 1 - c), False).start()

    for k in range(2):
        for side in (1, -1):
            zs, ok = each(a - 1, side)

            @pl.when(ok)
            def _():
                slot = at(zs, 1 - x, c)
                arrived(k, slot)
                copy(k, slot, 0, at(z, x, 1 - c), False).start()

    for k in range(2):
        owns[k].wait()
        for zs in range(a):
            for xs in range(2):
                arrived(k, at(zs, xs, 1 - c))
        ways(k, z, 0, 0, done)
        for d in range(1, a):
            for side in (1, -1):
                zs, ok = each(d, side)

                @pl.when(ok)
                def _():
                    ways(k, zs, d, side, done)

        for zs in range(a):
            copy(k, at(zs, 1 - x, c), 0, at(z, x, 1 - c), False).wait_send()


def gather(latents, keys, n):
    rows = latents.shape[0]
    hbm = pl.BlockSpec(memory_space=pl.ANY)
    return pl.pallas_call(
        functools.partial(gather_kernel, n),
        out_shape=(
            jax.ShapeDtypeStruct((n, rows, latents.shape[1]), BF16),
            jax.ShapeDtypeStruct((n, rows, keys.shape[1]), BF16),
        ),
        in_specs=[hbm, hbm],
        out_specs=(hbm, hbm),
        scratch_shapes=[
            pltpu.SemaphoreType.DMA((2, n, 4)),
            pltpu.SemaphoreType.DMA((2, n)),
            pltpu.SemaphoreType.DMA((2,)),
        ],
        compiler_params=pltpu.CompilerParams(collective_id=0, has_side_effects=True),
        name="gather",
    )(latents, keys)


def dot_t(a, b):
    return lax.dot_general(a, b, (((1,), (1,)), ((), ())), preferred_element_type=F32)


def index_kernel(heads, iq_ref, w_ref, key_ref, out_ref, scr):
    scr[...] = dot_t(iq_ref[...], key_ref[...])
    rows = []
    for t in range(TOK):
        acc = None
        for g in range(0, heads, 8):
            r = t * heads + g
            w = w_ref[r : r + 8, 0:1]
            part = jnp.maximum(scr[r : r + 8, :], 0.0) * w
            acc = part if acc is None else acc + part
        rows.append(jnp.sum(acc, axis=0, keepdims=True))
    out_ref[...] = jnp.concatenate(rows, axis=0)


def index_part(iq, wide, keys, heads):
    total, depth = iq.shape
    seq = keys.shape[0]
    m = TOK * heads
    return pl.pallas_call(
        functools.partial(index_kernel, heads),
        grid=(total // m,),
        out_shape=jax.ShapeDtypeStruct((total // heads, seq), F32),
        in_specs=[
            pl.BlockSpec((m, depth), lambda i: (i, 0)),
            pl.BlockSpec((m, wide.shape[1]), lambda i: (i, 0)),
            pl.BlockSpec((seq, depth), lambda i: (0, 0)),
        ],
        out_specs=pl.BlockSpec((TOK, seq), lambda i: (i, 0)),
        scratch_shapes=[pltpu.VMEM((m, seq), F32)],
        compiler_params=pltpu.CompilerParams(vmem_limit_bytes=VMEM_LIMIT),
        cost_estimate=pl.CostEstimate(
            flops=4 * total * seq * depth, bytes_accessed=4 * total * depth, transcendentals=0
        ),
        name="index_part",
    )(iq, wide, keys)


def attend_kernel(
    half, n, q_ref, lat_ref, pos_ref, mine_ref, out_ref, low_ref, scr_a, scr_b, bias, acc
):
    step = pl.program_id(0)
    seq = lat_ref.shape[0]
    lanes = q_ref.shape[2]
    count = lanes // 2
    rows = seq // n
    run = 64

    @pl.when(step == 0)
    def _():
        lane = lax.broadcasted_iota(jnp.int32, (rows, lanes), 1)
        row = lax.broadcasted_iota(jnp.int32, (rows, lanes), 0)
        mine = mine_ref[0] * rows + half * count + jnp.where(lane >= count, lane - count, lane)
        for b in range(n):
            seen = pos_ref[b] * rows + row <= mine
            bias[b * rows : (b + 1) * rows, :] = jnp.where(seen, 0.0, NEGATIVE)

    def scores(first):
        def part(h):
            return q_ref[h][:, half * count : (half + 1) * count]

        weights = jnp.concatenate([part(first + h) for h in range(4)], axis=1)
        return jnp.dot(lat_ref[...], weights, preferred_element_type=F32)

    def softmax(scr):
        scale = []
        for tile in (slice(0, lanes), slice(lanes, 2 * lanes)):
            top = None
            for r in range(0, seq, run):
                v = scr[r : r + run, tile] + bias[r : r + run, :]
                top = v if top is None else jnp.maximum(top, v)
            top = jnp.max(top, axis=0, keepdims=True)
            total = None
            for r in range(0, seq, run):
                v = scr[r : r + run, tile] + bias[r : r + run, :]
                p = jnp.exp2((v - top) * (SCALE_ATTN * LOG2E))
                scr[r : r + run, tile] = p
                total = p if total is None else total + p
            total = jnp.sum(total, axis=0, keepdims=True)
            scale.append(1.0 / (HEADS * total))
        for r in range(0, seq, run):
            acc[r : r + run, :] += (
                scr[r : r + run, :lanes] * scale[0] + scr[r : r + run, lanes:] * scale[1]
            )

    scr_a[...] = scores(0)
    softmax(scr_b)

    @pl.when(step == 0)
    def _():
        acc[...] = jnp.zeros_like(acc)

    scr_b[...] = scores(4)
    softmax(scr_a)

    @pl.when(step == pl.num_programs(0) - 1)
    def _():
        softmax(scr_b)
        both = jnp.transpose(acc[...])
        out = both[:count] + both[count:]
        out_ref[...] = out
        low_ref[...] = out.astype(BF16)


def attend(q, lat, block_pos, mine, half, n):
    heads, depth, lanes = q.shape
    seq = lat.shape[0]
    count = lanes // 2
    smem = pl.BlockSpec(memory_space=pltpu.SMEM)
    whole = lambda i: (0, 0)
    return pl.pallas_call(
        functools.partial(attend_kernel, half, n),
        grid=(heads // 8,),
        out_shape=(
            jax.ShapeDtypeStruct((count, seq), F32),
            jax.ShapeDtypeStruct((count, seq), BF16),
        ),
        in_specs=[
            pl.BlockSpec((8, depth, lanes), lambda i: (i, 0, 0)),
            pl.BlockSpec((seq, depth), whole),
            smem,
            smem,
        ],
        out_specs=(pl.BlockSpec((count, seq), whole), pl.BlockSpec((count, seq), whole)),
        scratch_shapes=[
            pltpu.VMEM((seq, 2 * lanes), F32),
            pltpu.VMEM((seq, 2 * lanes), F32),
            pltpu.VMEM((seq, lanes), F32),
            pltpu.VMEM((seq, lanes), F32),
        ],
        compiler_params=pltpu.CompilerParams(vmem_limit_bytes=VMEM_LIMIT),
        cost_estimate=pl.CostEstimate(
            flops=4 * count * heads * seq * depth,
            bytes_accessed=4 * count * heads * depth,
            transcendentals=count * heads * seq,
        ),
        name="attend",
    )(q, lat, block_pos, mine)


def back_kernel(heads, last, iq_ref, w_ref, key_ref, post_ref, poss_ref, *rest):
    peers_i = rest[0]
    own_i, own_t, peers_t = rest[1:4]
    gq_ref, gk_ref, scr, coef, acc, dscr = rest[-6:]
    step = pl.program_id(0)

    @pl.when(step == 0)
    def _():
        acc[...] = rest[4][...] if last else jnp.zeros_like(acc)

    scr[...] = dot_t(iq_ref[...], key_ref[...])
    index, target = own_i[...], own_t[...]
    for k in range(peers_i.shape[0]):
        index = index + peers_i[k]
        target = target + peers_t[k].astype(F32)
    seen = poss_ref[...] <= post_ref[...]
    masked = jnp.where(seen, index, NEGATIVE)
    weights = jnp.where(seen, jnp.exp(masked - jnp.max(masked, axis=1, keepdims=True)), 0.0)
    prob = weights * (1.0 / jnp.sum(weights, axis=1, keepdims=True))
    dscr[...] = jnp.where(seen, LOSS_SCALE * (prob - target), 0.0).astype(BF16).astype(F32)
    for t in range(TOK):
        for g in range(0, heads, 8):
            r = t * heads + g
            value = dscr[t : t + 1, :] * w_ref[r : r + 8, 0:1]
            coef[r : r + 8, :] = jnp.where(scr[r : r + 8, :] > 0.0, value, 0.0).astype(BF16)
    gq_ref[...] = jnp.dot(coef[...], key_ref[...], preferred_element_type=F32)
    acc[...] += lax.dot_general(
        iq_ref[...], coef[...], (((0,), (0,)), ((), ())), preferred_element_type=F32
    )

    @pl.when(step == pl.num_programs(0) - 1)
    def _():
        if last:
            gk_ref[...] = jnp.transpose(acc[...]).astype(BF16)
        else:
            gk_ref[...] = acc[...]


def back(iq, wide, keys, pos_t, pos_s, peers_i, own_i, own_t, peers_t, carried, heads, first, last):
    depth = iq.shape[1]
    seq = keys.shape[0]
    count = own_t.shape[0]
    m = TOK * heads
    off = first // TOK
    others = peers_i.shape[0]
    return pl.pallas_call(
        functools.partial(back_kernel, heads, last),
        grid=(count // TOK,),
        out_shape=(
            jax.ShapeDtypeStruct(iq.shape, F32),
            jax.ShapeDtypeStruct((seq, depth), BF16)
            if last
            else jax.ShapeDtypeStruct((depth, seq), F32),
        ),
        in_specs=[
            pl.BlockSpec((m, depth), lambda i: (i + off, 0)),
            pl.BlockSpec((m, wide.shape[1]), lambda i: (i + off, 0)),
            pl.BlockSpec((seq, depth), lambda i: (0, 0)),
            pl.BlockSpec((TOK, 1), lambda i: (i + off, 0)),
            pl.BlockSpec((1, seq), lambda i: (0, 0)),
            pl.BlockSpec((others, TOK, seq), lambda i: (0, i + off, 0)),
            pl.BlockSpec((TOK, seq), lambda i: (i + off, 0)),
            pl.BlockSpec((TOK, seq), lambda i: (i, 0)),
            pl.BlockSpec((others, TOK, seq), lambda i: (0, i, 0)),
        ]
        + [pl.BlockSpec((depth, seq), lambda i: (0, 0)), pl.BlockSpec(memory_space=pl.ANY)] * last,
        input_output_aliases={10: 0} if last else {},
        out_specs=(
            pl.BlockSpec((m, depth), lambda i: (i + off, 0)),
            pl.BlockSpec((seq, depth) if last else (depth, seq), lambda i: (0, 0)),
        ),
        scratch_shapes=[
            pltpu.VMEM((m, seq), F32),
            pltpu.VMEM((m, seq), BF16),
            pltpu.VMEM((depth, seq), F32),
            pltpu.VMEM((TOK, seq), F32),
        ],
        compiler_params=pltpu.CompilerParams(vmem_limit_bytes=VMEM_LIMIT),
        cost_estimate=pl.CostEstimate(
            flops=8 * count * heads * seq * depth,
            bytes_accessed=8 * count * heads * depth,
            transcendentals=0,
        ),
        name="back",
    )(iq, wide, keys, pos_t, pos_s, peers_i, own_i, own_t, peers_t, *carried)


def scatter_kernel(
    n, ranks, gk_ref, out_ref, got1, sum1, put2, got2, sum2, put3, got3, put4, got4, ssem, rsem
):
    z, x, c, a = place(n)
    y = lax.axis_index("head")
    barrier = pltpu.get_barrier_semaphore()
    greeted = [dict(ctx=at(z, 1 - x, c)), dict(ctx=at(z, x, 1 - c))]
    greeted += [dict(ctx=at(lax.rem(z + d, a), x, c)) for d in range(1, a)]
    greeted += [dict(head=lax.rem(y + d, ranks)) for d in range(1, ranks)]
    for where in greeted:
        pl.semaphore_signal(barrier, inc=1, device_id=where, device_id_type=MESH)
    pl.semaphore_wait(barrier, len(greeted))

    first = remote(gk_ref.at[:, :, 1 - c], got1, ssem.at[0], rsem.at[0], ctx=at(z, x, 1 - c))
    first.start()
    first.wait()
    sum1[...] = gk_ref[:, :, c].astype(F32) + got1[...].astype(F32)
    put2[...] = sum1[:, 1 - x].astype(BF16)
    second = remote(put2, got2, ssem.at[1], rsem.at[1], ctx=at(z, 1 - x, c))
    second.start()
    second.wait()
    sum2[...] = sum1[:, x] + got2[...].astype(F32)
    put3[...] = sum2[...].astype(BF16)
    third = []
    for d in range(1, a):
        to = lax.rem(z + d, a)
        item = remote(
            put3.at[to], got3.at[d - 1], ssem.at[1 + d], rsem.at[1 + d], ctx=at(to, x, c)
        )
        item.start()
        third.append(item)
    for item in third:
        item.wait()
    part = sum2[z]
    for d in range(1, a):
        part = part + got3[d - 1].astype(F32)
    put4[...] = part
    fourth = []
    for d in range(1, ranks):
        item = remote(
            put4,
            got4.at[d - 1],
            ssem.at[a + d],
            rsem.at[a + d],
            head=lax.rem(y + d, ranks),
        )
        item.start()
        fourth.append(item)
    for item in fourth:
        item.wait()
    part = put4[...]
    for d in range(1, ranks):
        part = part + got4[d - 1]
    out_ref[...] = part


def scatter(gk, n, ranks):
    a = n // 4
    rows, depth = gk.shape[0] // n, gk.shape[1]
    vmem = pl.BlockSpec(memory_space=pltpu.VMEM)
    return pl.pallas_call(
        functools.partial(scatter_kernel, n, ranks),
        out_shape=jax.ShapeDtypeStruct((rows, depth), F32),
        in_specs=[vmem],
        out_specs=vmem,
        scratch_shapes=[
            pltpu.VMEM((a, 2, rows, depth), BF16),
            pltpu.VMEM((a, 2, rows, depth), F32),
            pltpu.VMEM((a, rows, depth), BF16),
            pltpu.VMEM((a, rows, depth), BF16),
            pltpu.VMEM((a, rows, depth), F32),
            pltpu.VMEM((a, rows, depth), BF16),
            pltpu.VMEM((a - 1, rows, depth), BF16),
            pltpu.VMEM((rows, depth), F32),
            pltpu.VMEM((ranks - 1, rows, depth), F32),
            pltpu.SemaphoreType.DMA((a + ranks,)),
            pltpu.SemaphoreType.DMA((a + ranks,)),
        ],
        compiler_params=pltpu.CompilerParams(collective_id=1, has_side_effects=True),
        name="scatter",
    )(gk.reshape(a, 2, 2, rows, depth))


def swap(value, ranks):
    return jnp.stack(
        [
            lax.ppermute(value, "head", [(i, (i + d) % ranks) for i in range(ranks)])
            for d in range(1, ranks)
        ]
    )


def body(queries, latents, index_queries, index_keys, head_weights, block_pos):
    rows, heads, rank = queries.shape
    depth = index_queries.shape[2]
    n, ranks = lax.axis_size("ctx"), lax.axis_size("head")
    seq = rows * n
    q = jnp.transpose(queries, (1, 2, 0))
    iq = index_queries.reshape(rows * heads, depth)
    wide = jnp.broadcast_to(
        (head_weights * depth ** (-0.5))[:, :, None], (rows, heads, 128)
    ).reshape(rows * heads, 128)
    local = jnp.arange(rows, dtype=jnp.int32)
    pos_s = (block_pos[:, None] * rows + local[None, :]).reshape(1, seq)
    mine = jnp.sum(jnp.where(jnp.arange(n) == lax.axis_index("ctx"), block_pos, 0))
    pos_t = (mine * rows + local)[:, None]

    lat, keys = gather(latents, index_keys, n)
    lat = lat.reshape(seq, rank)
    keys = keys.reshape(seq, depth)
    own_i = index_part(iq, wide, keys, heads)
    peers_i = swap(own_i, ranks)
    own_t, peers_t = [], []
    for k in range(2):
        full, low = attend(q, lat, block_pos, mine[None], k, n)
        own_t.append(full)
        peers_t.append(swap(low, ranks))
    grads = ()
    for k in range(2):
        grad_queries, carry = back(
            iq, wide, keys, pos_t, pos_s, peers_i, own_i, own_t[k], peers_t[k], grads, heads,
            k * (rows // 2), k == 1,
        )
        grads = (carry, grad_queries)
    return grad_queries.reshape(rows, heads, depth), scatter(carry, n, ranks)


def solution(mesh):
    return jax.shard_map(
        body,
        mesh=mesh,
        in_specs=(
            P("ctx", "head", None),
            P("ctx", None),
            P("ctx", "head", None),
            P("ctx", None),
            P("ctx", "head"),
            P(),
        ),
        out_specs=(P("ctx", "head", None), P("ctx", None)),
        check_vma=False,
    )
```

```python
import functools
import math

import jax
import jax.numpy as jnp
from jax import lax
from jax.experimental import pallas as pl
from jax.experimental.pallas import tpu as pltpu
from jax.sharding import PartitionSpec as P

HEADS = 64
SCALE_ATTN = 192.0 ** (-0.5)
LOSS_SCALE = 1024.0
NEGATIVE = -1e30
LOG2E = math.log2(math.e)
MESH = pl.DeviceIdType.MESH
F32 = jnp.float32
BF16 = jnp.bfloat16
TOK = 8
ITOK = 8
PIECES = 8
VMEM_LIMIT = 60 * 1024 * 1024


def place(n):
    me = lax.axis_index("ctx")
    a = n // 4
    return me // 4, (me // 2) % 2, me % 2, a


def at(z, x, c):
    return (z * 2 + x) * 2 + c


def remote(src, dst, send, recv, **where):
    return pltpu.make_async_remote_copy(
        src_ref=src, dst_ref=dst, send_sem=send, recv_sem=recv, device_id=where, device_id_type=MESH
    )


def dot_t(a, b):
    return lax.dot_general(a, b, (((1,), (1,)), ((), ())), preferred_element_type=F32)


def gather_kernel(
    n, heads, lat_ref, key_ref, iq_ref, w_ref, lat_out, key_out, idx_ref,
    scr_a, scr_b, send_sem, recv_sem, own_sem,
):
    z, x, c, a = place(n)
    y = lax.axis_index("head")
    other_y = y + 1 - 2 * (y % 2)
    up, down = z + 1 < a, z > 0
    partner = at(z, x, 1 - c)
    barrier = pltpu.get_barrier_semaphore()

    def greet(**where):
        pl.semaphore_signal(barrier, inc=1, device_id=where, device_id_type=MESH)

    greet(ctx=at(z, 1 - x, c))
    greet(ctx=partner)
    greet(head=other_y)

    @pl.when(up)
    def _():
        greet(ctx=at(z + 1, x, c))

    @pl.when(down)
    def _():
        greet(ctx=at(z - 1, x, c))

    me = at(z, x, c)
    owns = []
    for k, (src, dst) in enumerate(((key_ref, key_out), (lat_ref, lat_out))):
        own = pltpu.make_async_copy(src, dst.at[me], own_sem.at[k])
        own.start()
        owns.append(own)
    pl.semaphore_wait(barrier, 3 + up.astype(jnp.int32) + down.astype(jnp.int32))

    rows = lat_ref.shape[0]
    part = rows // 2

    def piece(ref, k):
        return ref.at[pl.ds(pl.multiple_of((k - 1) * part, part), part)]

    def copy(k, slot, way, first, **where):
        if isinstance(k, int) and k == 0:
            src, dst = (key_ref if first else key_out.at[slot]), key_out.at[slot]
        else:
            dst = piece(lat_out.at[slot], k)
            src = piece(lat_ref, k) if first else dst
        return remote(src, dst, send_sem.at[k, slot, way], recv_sem.at[k, slot], **where)

    def to_core(k, slot, first=False):
        return copy(k, slot, 0, first, ctx=partner)

    def to_x(k, slot, first=False):
        return copy(k, slot, 1, first, ctx=at(z, 1 - x, c))

    def to_y(k, slot):
        return copy(k, slot, 4, False, head=other_y)

    def arrived(k, slot):
        to_core(k, slot).wait_recv()

    def line(k, slot, first, side, act):
        if side >= 0:

            @pl.when(up)
            def _():
                act(copy(k, slot, 2, first, ctx=at(z + 1, x, c)))

        if side <= 0:

            @pl.when(down)
            def _():
                act(copy(k, slot, 3, first, ctx=at(z - 1, x, c)))

    def sides(d, act):
        for side in (1, -1) if d > 0 else (0,):
            zs = z - d if side >= 0 else z + d
            if d == 0:
                act(zs, side)
            else:
                ok = zs >= 0 if side > 0 else zs < a
                pl.when(ok)(functools.partial(act, zs, side))

    start = lambda item: item.start()
    done = lambda item: item.wait_send()
    mine, others = 1 + y % 2, 2 - y % 2

    def column(ks, d, wait, act):
        def go(zs, side):
            slot = at(zs, x, c)
            for k in ks:
                if wait and d > 0:
                    arrived(k, slot)
                line(k, slot, d == 0, side, act)
            crossing = 0 if ks == (0,) else mine
            act(to_x(crossing, slot, d == 0))
            for k in ks:
                act(to_core(k, slot, d == 0))

        sides(d, go)

    def crossed(k, d, wait, act, onward):
        def go(zs, side):
            slot = at(zs, 1 - x, c)
            if wait:
                arrived(k, slot)
            if onward:
                act(to_y(k, slot))
            act(to_core(k, slot))

        sides(d, go)

    column((0,), 0, True, start)
    column((1, 2), 0, True, start)
    for d in range(1, a):
        column((0,), d, True, start)
        crossed(0, d - 1, True, start, False)
    crossed(0, a - 1, True, start, False)

    owns[0].wait()
    for zs in range(a):
        for xs in range(2):
            arrived(0, at(zs, xs, 1 - c))

    def stage(d):
        if d < a:
            column((1, 2), d, True, start)
        if 1 <= d <= a:
            crossed(mine, d - 1, True, start, True)
        if 2 <= d:
            crossed(others, d - 2, True, start, False)

    depth = iq_ref.shape[1]
    m = ITOK * heads
    width = 4 * rows

    def index_chunk(i, _):
        iq = iq_ref[pl.ds(pl.multiple_of(i * m, m), m), :]
        w = w_ref.at[pl.ds(pl.multiple_of(i * m, m), m)]
        out = idx_ref.at[pl.ds(pl.multiple_of(i * ITOK, ITOK), ITOK)]
        scrs = (scr_a, scr_b)

        def reduce(p):
            scr = scrs[p % 2]
            sums = []
            for t in range(ITOK):
                acc = None
                for g in range(0, heads, 8):
                    r = t * heads + g
                    term = jnp.maximum(scr[r : r + 8, :], 0.0) * w[r : r + 8, 0:1]
                    acc = term if acc is None else acc + term
                sums.append(jnp.sum(acc, axis=0, keepdims=True))
            out[:, p * width : (p + 1) * width] = jnp.concatenate(sums, axis=0)

        count = n * rows // width
        per = width // rows
        for p in range(count):
            held = key_out[p * per : (p + 1) * per].reshape(width, depth)
            scrs[p % 2][...] = dot_t(iq, held)
            if p > 0:
                reduce(p - 1)
        reduce(count - 1)
        return 0

    chunks = iq_ref.shape[0] // m
    cut = [chunks * d // (a + 2) for d in range(a + 3)]
    for d in range(a + 2):
        lax.fori_loop(cut[d], cut[d + 1], index_chunk, 0)
        if d + 1 < a + 2:
            stage(d + 1)

    owns[1].wait()
    for zs in range(a):
        for xs in range(2):
            for k in (1, 2):
                arrived(k, at(zs, xs, 1 - c))
    for ks in ((0,), (1, 2)):
        for d in range(a):
            column(ks, d, False, done)
    for d in range(a):
        crossed(0, d, False, done, False)
        crossed(mine, d, False, done, True)
        crossed(others, d, False, done, False)


def gather(latents, keys, iq, wide, heads, n):
    rows = latents.shape[0]
    seq = rows * n
    hbm = pl.BlockSpec(memory_space=pl.ANY)
    vmem = pl.BlockSpec(memory_space=pltpu.VMEM)
    m = ITOK * heads
    return pl.pallas_call(
        functools.partial(gather_kernel, n, heads),
        out_shape=(
            jax.ShapeDtypeStruct((n, rows, latents.shape[1]), BF16),
            jax.ShapeDtypeStruct((n, rows, keys.shape[1]), BF16),
            jax.ShapeDtypeStruct((iq.shape[0] // heads, seq), F32),
        ),
        in_specs=[hbm, hbm, vmem, vmem],
        out_specs=(hbm, vmem, vmem),
        scratch_shapes=[
            pltpu.VMEM((m, 4 * rows), F32),
            pltpu.VMEM((m, 4 * rows), F32),
            pltpu.SemaphoreType.DMA((3, n, 5)),
            pltpu.SemaphoreType.DMA((3, n)),
            pltpu.SemaphoreType.DMA((2,)),
        ],
        compiler_params=pltpu.CompilerParams(
            collective_id=0, has_side_effects=True, vmem_limit_bytes=VMEM_LIMIT
        ),
        name="gather",
    )(latents, keys, iq, wide)


def attend_kernel(
    half, n, q_ref, lat_ref, pos_ref, mine_ref, out_ref, low_ref, scr_a, scr_b, bias, acc
):
    step = pl.program_id(0)
    seq = lat_ref.shape[0]
    lanes = q_ref.shape[2]
    count = lanes // 2
    rows = seq // n
    run = 64

    @pl.when(step == 0)
    def _():
        lane = lax.broadcasted_iota(jnp.int32, (rows, lanes), 1)
        row = lax.broadcasted_iota(jnp.int32, (rows, lanes), 0)
        mine = mine_ref[0] * rows + half * count + jnp.where(lane >= count, lane - count, lane)
        for b in range(n):
            seen = pos_ref[b] * rows + row <= mine
            bias[b * rows : (b + 1) * rows, :] = jnp.where(seen, 0.0, NEGATIVE)

    def scores(first, scr):
        def part(h):
            return q_ref[h][:, half * count : (half + 1) * count]

        weights = jnp.concatenate([part(first + h) for h in range(4)], axis=1)
        piece = seq // PIECES
        for r in range(0, seq, piece):
            scr[r : r + piece, :] = jnp.dot(
                lat_ref[r : r + piece, :], weights, preferred_element_type=F32
            )
            yield

    def softmax(scr):
        scale = []
        for tile in (slice(0, lanes), slice(lanes, 2 * lanes)):
            top = None
            for r in range(0, seq, run):
                v = scr[r : r + run, tile] + bias[r : r + run, :]
                top = v if top is None else jnp.maximum(top, v)
                yield
            top = jnp.max(top, axis=0, keepdims=True)
            total = None
            for r in range(0, seq, run):
                v = scr[r : r + run, tile] + bias[r : r + run, :]
                p = jnp.exp2((v - top) * (SCALE_ATTN * LOG2E))
                scr[r : r + run, tile] = p
                total = p if total is None else total + p
                yield
            total = jnp.sum(total, axis=0, keepdims=True)
            scale.append(1.0 / (HEADS * total))
        for r in range(0, seq, run):
            acc[r : r + run, :] += (
                scr[r : r + run, :lanes] * scale[0] + scr[r : r + run, lanes:] * scale[1]
            )
            yield

    def together(dots, vectors):
        per = -(-5 * (seq // run) // PIECES)
        for _ in dots:
            for _ in range(per):
                next(vectors, None)
        for _ in vectors:
            pass

    together(scores(0, scr_a), softmax(scr_b))

    @pl.when(step == 0)
    def _():
        acc[...] = jnp.zeros_like(acc)

    together(scores(4, scr_b), softmax(scr_a))

    @pl.when(step == pl.num_programs(0) - 1)
    def _():
        for _ in softmax(scr_b):
            pass
        both = jnp.transpose(acc[...])
        out = both[:count] + both[count:]
        out_ref[...] = out
        low_ref[...] = out.astype(BF16)


def attend(q, lat, block_pos, mine, half, n):
    heads, depth, lanes = q.shape
    seq = lat.shape[0]
    count = lanes // 2
    smem = pl.BlockSpec(memory_space=pltpu.SMEM)
    whole = lambda i: (0, 0)
    return pl.pallas_call(
        functools.partial(attend_kernel, half, n),
        grid=(heads // 8,),
        out_shape=(
            jax.ShapeDtypeStruct((count, seq), F32),
            jax.ShapeDtypeStruct((count, seq), BF16),
        ),
        in_specs=[
            pl.BlockSpec((8, depth, lanes), lambda i: (i, 0, 0)),
            pl.BlockSpec((seq, depth), whole),
            smem,
            smem,
        ],
        out_specs=(pl.BlockSpec((count, seq), whole), pl.BlockSpec((count, seq), whole)),
        scratch_shapes=[
            pltpu.VMEM((seq, 2 * lanes), F32),
            pltpu.VMEM((seq, 2 * lanes), F32),
            pltpu.VMEM((seq, lanes), F32),
            pltpu.VMEM((seq, lanes), F32),
        ],
        compiler_params=pltpu.CompilerParams(vmem_limit_bytes=VMEM_LIMIT),
        cost_estimate=pl.CostEstimate(
            flops=4 * count * heads * seq * depth,
            bytes_accessed=4 * count * heads * depth,
            transcendentals=count * heads * seq,
        ),
        name="attend",
    )(q, lat, block_pos, mine)


def back_kernel(heads, last, iq_ref, w_ref, key_ref, post_ref, poss_ref, *rest):
    peers_i = rest[0]
    own_i, own_t, peers_t = rest[1:4]
    gq_ref, gk_ref, scr, coef, acc, dscr = rest[-6:]
    step = pl.program_id(0)

    @pl.when(step == 0)
    def _():
        acc[...] = rest[4][...] if last else jnp.zeros_like(acc)

    scr[...] = dot_t(iq_ref[...], key_ref[...])
    index, target = own_i[...], own_t[...]
    for k in range(peers_i.shape[0]):
        index = index + peers_i[k]
        target = target + peers_t[k].astype(F32)
    seen = poss_ref[...] <= post_ref[...]
    masked = jnp.where(seen, index, NEGATIVE)
    weights = jnp.where(seen, jnp.exp(masked - jnp.max(masked, axis=1, keepdims=True)), 0.0)
    prob = weights * (1.0 / jnp.sum(weights, axis=1, keepdims=True))
    dscr[...] = jnp.where(seen, LOSS_SCALE * (prob - target), 0.0).astype(BF16).astype(F32)
    for t in range(TOK):
        for g in range(0, heads, 8):
            r = t * heads + g
            value = dscr[t : t + 1, :] * w_ref[r : r + 8, 0:1]
            coef[r : r + 8, :] = jnp.where(scr[r : r + 8, :] > 0.0, value, 0.0).astype(BF16)
    gq_ref[...] = jnp.dot(coef[...], key_ref[...], preferred_element_type=F32)
    acc[...] += lax.dot_general(
        iq_ref[...], coef[...], (((0,), (0,)), ((), ())), preferred_element_type=F32
    )

    @pl.when(step == pl.num_programs(0) - 1)
    def _():
        if last:
            gk_ref[...] = jnp.transpose(acc[...]).astype(BF16)
        else:
            gk_ref[...] = acc[...]


def back(iq, wide, keys, pos_t, pos_s, peers_i, own_i, own_t, peers_t, carried, heads, first, last):
    depth = iq.shape[1]
    seq = keys.shape[0]
    count = own_t.shape[0]
    m = TOK * heads
    off = first // TOK
    others = peers_i.shape[0]
    return pl.pallas_call(
        functools.partial(back_kernel, heads, last),
        grid=(count // TOK,),
        out_shape=(
            jax.ShapeDtypeStruct(iq.shape, F32),
            jax.ShapeDtypeStruct((seq, depth), BF16)
            if last
            else jax.ShapeDtypeStruct((depth, seq), F32),
        ),
        in_specs=[
            pl.BlockSpec((m, depth), lambda i: (i + off, 0)),
            pl.BlockSpec((m, wide.shape[1]), lambda i: (i + off, 0)),
            pl.BlockSpec((seq, depth), lambda i: (0, 0)),
            pl.BlockSpec((TOK, 1), lambda i: (i + off, 0)),
            pl.BlockSpec((1, seq), lambda i: (0, 0)),
            pl.BlockSpec((others, TOK, seq), lambda i: (0, i + off, 0)),
            pl.BlockSpec((TOK, seq), lambda i: (i + off, 0)),
            pl.BlockSpec((TOK, seq), lambda i: (i, 0)),
            pl.BlockSpec((others, TOK, seq), lambda i: (0, i, 0)),
        ]
        + [pl.BlockSpec((depth, seq), lambda i: (0, 0)), pl.BlockSpec(memory_space=pl.ANY)] * last,
        input_output_aliases={10: 0} if last else {},
        out_specs=(
            pl.BlockSpec((m, depth), lambda i: (i + off, 0)),
            pl.BlockSpec((seq, depth) if last else (depth, seq), lambda i: (0, 0)),
        ),
        scratch_shapes=[
            pltpu.VMEM((m, seq), F32),
            pltpu.VMEM((m, seq), BF16),
            pltpu.VMEM((depth, seq), F32),
            pltpu.VMEM((TOK, seq), F32),
        ],
        compiler_params=pltpu.CompilerParams(vmem_limit_bytes=VMEM_LIMIT),
        cost_estimate=pl.CostEstimate(
            flops=8 * count * heads * seq * depth,
            bytes_accessed=8 * count * heads * depth,
            transcendentals=0,
        ),
        name="back",
    )(iq, wide, keys, pos_t, pos_s, peers_i, own_i, own_t, peers_t, *carried)


def scatter_kernel(
    n, ranks, gk_ref, out_ref, got1, sum1, put2, got2, sum2, put3, got3, put4, got4, ssem, rsem
):
    z, x, c, a = place(n)
    y = lax.axis_index("head")
    barrier = pltpu.get_barrier_semaphore()
    greeted = [dict(ctx=at(z, 1 - x, c)), dict(ctx=at(z, x, 1 - c))]
    greeted += [dict(ctx=at(lax.rem(z + d, a), x, c)) for d in range(1, a)]
    greeted += [dict(head=lax.rem(y + d, ranks)) for d in range(1, ranks)]
    for where in greeted:
        pl.semaphore_signal(barrier, inc=1, device_id=where, device_id_type=MESH)
    pl.semaphore_wait(barrier, len(greeted))

    first = remote(gk_ref.at[:, :, 1 - c], got1, ssem.at[0], rsem.at[0], ctx=at(z, x, 1 - c))
    first.start()
    first.wait()
    sum1[...] = gk_ref[:, :, c].astype(F32) + got1[...].astype(F32)
    put2[...] = sum1[:, 1 - x].astype(BF16)
    second = remote(put2, got2, ssem.at[1], rsem.at[1], ctx=at(z, 1 - x, c))
    second.start()
    second.wait()
    sum2[...] = sum1[:, x] + got2[...].astype(F32)
    put3[...] = sum2[...].astype(BF16)
    third = []
    for d in range(1, a):
        to = lax.rem(z + d, a)
        item = remote(
            put3.at[to], got3.at[d - 1], ssem.at[1 + d], rsem.at[1 + d], ctx=at(to, x, c)
        )
        item.start()
        third.append(item)
    for item in third:
        item.wait()
    part = sum2[z]
    for d in range(1, a):
        part = part + got3[d - 1].astype(F32)
    put4[...] = part
    fourth = []
    for d in range(1, ranks):
        item = remote(
            put4,
            got4.at[d - 1],
            ssem.at[a + d],
            rsem.at[a + d],
            head=lax.rem(y + d, ranks),
        )
        item.start()
        fourth.append(item)
    for item in fourth:
        item.wait()
    part = put4[...]
    for d in range(1, ranks):
        part = part + got4[d - 1]
    out_ref[...] = part


def scatter(gk, n, ranks):
    a = n // 4
    rows, depth = gk.shape[0] // n, gk.shape[1]
    vmem = pl.BlockSpec(memory_space=pltpu.VMEM)
    return pl.pallas_call(
        functools.partial(scatter_kernel, n, ranks),
        out_shape=jax.ShapeDtypeStruct((rows, depth), F32),
        in_specs=[vmem],
        out_specs=vmem,
        scratch_shapes=[
            pltpu.VMEM((a, 2, rows, depth), BF16),
            pltpu.VMEM((a, 2, rows, depth), F32),
            pltpu.VMEM((a, rows, depth), BF16),
            pltpu.VMEM((a, rows, depth), BF16),
            pltpu.VMEM((a, rows, depth), F32),
            pltpu.VMEM((a, rows, depth), BF16),
            pltpu.VMEM((a - 1, rows, depth), BF16),
            pltpu.VMEM((rows, depth), F32),
            pltpu.VMEM((ranks - 1, rows, depth), F32),
            pltpu.SemaphoreType.DMA((a + ranks,)),
            pltpu.SemaphoreType.DMA((a + ranks,)),
        ],
        compiler_params=pltpu.CompilerParams(collective_id=1, has_side_effects=True),
        name="scatter",
    )(gk.reshape(a, 2, 2, rows, depth))


def swap(value, ranks):
    return jnp.stack(
        [
            lax.ppermute(value, "head", [(i, (i + d) % ranks) for i in range(ranks)])
            for d in range(1, ranks)
        ]
    )


def body(queries, latents, index_queries, index_keys, head_weights, block_pos):
    rows, heads, rank = queries.shape
    depth = index_queries.shape[2]
    n, ranks = lax.axis_size("ctx"), lax.axis_size("head")
    seq = rows * n
    q = jnp.transpose(queries, (1, 2, 0))
    iq = index_queries.reshape(rows * heads, depth)
    wide = jnp.broadcast_to(
        (head_weights * depth ** (-0.5))[:, :, None], (rows, heads, 128)
    ).reshape(rows * heads, 128)
    local = jnp.arange(rows, dtype=jnp.int32)
    pos_s = (block_pos[:, None] * rows + local[None, :]).reshape(1, seq)
    mine = jnp.sum(jnp.where(jnp.arange(n) == lax.axis_index("ctx"), block_pos, 0))
    pos_t = (mine * rows + local)[:, None]

    lat, keys, own_i = gather(latents, index_keys, iq, wide, heads, n)
    lat = lat.reshape(seq, rank)
    keys = keys.reshape(seq, depth)
    peers_i = swap(own_i, ranks)
    own_t, peers_t = [], []
    for k in range(2):
        full, low = attend(q, lat, block_pos, mine[None], k, n)
        own_t.append(full)
        peers_t.append(swap(low, ranks))
    grads = ()
    for k in range(2):
        grad_queries, carry = back(
            iq, wide, keys, pos_t, pos_s, peers_i, own_i, own_t[k], peers_t[k], grads, heads,
            k * (rows // 2), k == 1,
        )
        grads = (carry, grad_queries)
    return grad_queries.reshape(rows, heads, depth), scatter(carry, n, ranks)


def solution(mesh):
    return jax.shard_map(
        body,
        mesh=mesh,
        in_specs=(
            P("ctx", "head", None),
            P("ctx", None),
            P("ctx", "head", None),
            P("ctx", None),
            P("ctx", "head"),
            P(),
        ),
        out_specs=(P("ctx", "head", None), P("ctx", None)),
        check_vma=False,
    )
```

```python
import functools
import math

import jax
import jax.numpy as jnp
from jax import lax
from jax.experimental import pallas as pl
from jax.experimental.pallas import tpu as pltpu
from jax.sharding import PartitionSpec as P

HEADS = 64
SCALE_ATTN = 192.0 ** (-0.5)
LOSS_SCALE = 1024.0
NEGATIVE = -1e30
LOG2E = math.log2(math.e)
MESH = pl.DeviceIdType.MESH
F32 = jnp.float32
BF16 = jnp.bfloat16
TOK = 8
ITOK = 8
PIECES = 8
VMEM_LIMIT = 60 * 1024 * 1024


def place(n):
    me = lax.axis_index("ctx")
    a = n // 4
    return me // 4, (me // 2) % 2, me % 2, a


def at(z, x, c):
    return (z * 2 + x) * 2 + c


def remote(src, dst, send, recv, **where):
    return pltpu.make_async_remote_copy(
        src_ref=src, dst_ref=dst, send_sem=send, recv_sem=recv, device_id=where, device_id_type=MESH
    )


def dot_t(a, b):
    return lax.dot_general(a, b, (((1,), (1,)), ((), ())), preferred_element_type=F32)


def gather_kernel(
    n, heads, lat_ref, key_ref, iq_ref, w_ref, lat_out, key_out, idx_ref,
    scr_a, scr_b, send_sem, recv_sem, own_sem,
):
    z, x, c, a = place(n)
    y = lax.axis_index("head")
    other_y = y + 1 - 2 * (y % 2)
    partner = at(z, x, 1 - c)
    barrier = pltpu.get_barrier_semaphore()

    def greet(**where):
        pl.semaphore_signal(barrier, inc=1, device_id=where, device_id_type=MESH)

    greet(ctx=at(z, 1 - x, c))
    greet(ctx=partner)
    greet(head=other_y)

    for d in range(1, a):
        greet(ctx=at((z + d) % a, x, c))

    me = at(z, x, c)
    owns = []
    for k, (src, dst) in enumerate(((key_ref, key_out), (lat_ref, lat_out))):
        own = pltpu.make_async_copy(src, dst.at[me], own_sem.at[k])
        own.start()
        owns.append(own)
    pl.semaphore_wait(barrier, 2 + a)

    rows = lat_ref.shape[0]
    part = rows // 2

    def piece(ref, k):
        return ref.at[pl.ds(pl.multiple_of((k - 1) * part, part), part)]

    def copy(k, slot, way, first, **where):
        if isinstance(k, int) and k == 0:
            src, dst = (key_ref if first else key_out.at[slot]), key_out.at[slot]
        else:
            dst = piece(lat_out.at[slot], k)
            src = piece(lat_ref, k) if first else dst
        return remote(src, dst, send_sem.at[k, slot, way], recv_sem.at[k, slot], **where)

    def to_core(k, slot, first=False):
        return copy(k, slot, 0, first, ctx=partner)

    def to_x(k, slot, first=False):
        return copy(k, slot, 1, first, ctx=at(z, 1 - x, c))

    def to_y(k, slot):
        return copy(k, slot, 2, False, head=other_y)

    def arrived(k, slot):
        to_core(k, slot).wait_recv()

    def line(k, slot, act):
        for d in range(1, a):
            act(copy(k, slot, 4 + d, True, ctx=at((z + d) % a, x, c)))

    def sides(d, act):
        for side in (1, -1) if d > 0 else (0,):
            zs = z - d if side >= 0 else z + d
            if d == 0:
                act(zs, side)
            else:
                ok = zs >= 0 if side > 0 else zs < a
                pl.when(ok)(functools.partial(act, zs, side))

    start = lambda item: item.start()
    done = lambda item: item.wait_send()
    mine, others = 1 + y % 2, 2 - y % 2

    def column(ks, d, wait, act):
        def go(zs, side):
            slot = at(zs, x, c)
            for k in ks:
                if wait and d > 0:
                    arrived(k, slot)
                if d == 0:
                    line(k, slot, act)
            crossing = 0 if ks == (0,) else mine
            act(to_x(crossing, slot, d == 0))
            for k in ks:
                act(to_core(k, slot, d == 0))

        sides(d, go)

    def crossed(k, d, wait, act, onward):
        def go(zs, side):
            slot = at(zs, 1 - x, c)
            if wait:
                arrived(k, slot)
            if onward:
                act(to_y(k, slot))
            act(to_core(k, slot))

        sides(d, go)

    column((0,), 0, True, start)
    for d in range(1, a):
        column((0,), d, True, start)
    column((1, 2), 0, True, start)
    for d in range(a):
        crossed(0, d, True, start, False)

    owns[0].wait()
    for zs in range(a):
        for xs in range(2):
            arrived(0, at(zs, xs, 1 - c))

    stages = []
    for d in range(a + 2):
        if 1 <= d < a:
            stages.append(functools.partial(column, (1, 2), d, True, start))
        if 1 <= d <= a:
            stages.append(functools.partial(crossed, mine, d - 1, True, start, True))
        if 2 <= d:
            stages.append(functools.partial(crossed, others, d - 2, True, start, False))

    depth = iq_ref.shape[1]
    m = ITOK * heads
    width = 4 * rows

    def index_chunk(i, _):
        iq = iq_ref[pl.ds(pl.multiple_of(i * m, m), m), :]
        w = w_ref.at[pl.ds(pl.multiple_of(i * m, m), m)]
        out = idx_ref.at[pl.ds(pl.multiple_of(i * ITOK, ITOK), ITOK)]
        scrs = (scr_a, scr_b)

        def reduce(p):
            scr = scrs[p % 2]
            sums = []
            for t in range(ITOK):
                acc = None
                for g in range(0, heads, 8):
                    r = t * heads + g
                    term = jnp.maximum(scr[r : r + 8, :], 0.0) * w[r : r + 8, 0:1]
                    acc = term if acc is None else acc + term
                sums.append(jnp.sum(acc, axis=0, keepdims=True))
            out[:, p * width : (p + 1) * width] = jnp.concatenate(sums, axis=0)

        count = n * rows // width
        per = width // rows
        for p in range(count):
            held = key_out[p * per : (p + 1) * per].reshape(width, depth)
            scrs[p % 2][...] = dot_t(iq, held)
            if p > 0:
                reduce(p - 1)
        reduce(count - 1)
        return 0

    chunks = iq_ref.shape[0] // m
    lead = chunks // 4
    count = len(stages)
    cut = [0] + [lead + (chunks - lead) * d // count for d in range(count)] + [chunks]
    for d in range(count + 1):
        if cut[d + 1] > cut[d]:
            lax.fori_loop(cut[d], cut[d + 1], index_chunk, 0)
        if d < count:
            stages[d]()

    owns[1].wait()
    for zs in range(a):
        for xs in range(2):
            for k in (1, 2):
                arrived(k, at(zs, xs, 1 - c))
    for ks in ((0,), (1, 2)):
        for d in range(a):
            column(ks, d, False, done)
    for d in range(a):
        crossed(0, d, False, done, False)
        crossed(mine, d, False, done, True)
        crossed(others, d, False, done, False)


def gather(latents, keys, iq, wide, heads, n):
    rows = latents.shape[0]
    seq = rows * n
    hbm = pl.BlockSpec(memory_space=pl.ANY)
    vmem = pl.BlockSpec(memory_space=pltpu.VMEM)
    m = ITOK * heads
    return pl.pallas_call(
        functools.partial(gather_kernel, n, heads),
        out_shape=(
            jax.ShapeDtypeStruct((n, rows, latents.shape[1]), BF16),
            jax.ShapeDtypeStruct((n, rows, keys.shape[1]), BF16),
            jax.ShapeDtypeStruct((iq.shape[0] // heads, seq), F32),
        ),
        in_specs=[hbm, hbm, vmem, vmem],
        out_specs=(hbm, vmem, vmem),
        scratch_shapes=[
            pltpu.VMEM((m, 4 * rows), F32),
            pltpu.VMEM((m, 4 * rows), F32),
            pltpu.SemaphoreType.DMA((3, n, 4 + n // 4)),
            pltpu.SemaphoreType.DMA((3, n)),
            pltpu.SemaphoreType.DMA((2,)),
        ],
        compiler_params=pltpu.CompilerParams(
            collective_id=0, has_side_effects=True, vmem_limit_bytes=VMEM_LIMIT
        ),
        name="gather",
    )(latents, keys, iq, wide)


def attend_kernel(
    half, n, q_ref, lat_ref, pos_ref, mine_ref, out_ref, low_ref, scr_a, scr_b, bias, acc
):
    step = pl.program_id(0)
    seq = lat_ref.shape[0]
    lanes = q_ref.shape[2]
    count = lanes // 2
    rows = seq // n
    run = 64

    @pl.when(step == 0)
    def _():
        lane = lax.broadcasted_iota(jnp.int32, (rows, lanes), 1)
        row = lax.broadcasted_iota(jnp.int32, (rows, lanes), 0)
        mine = mine_ref[0] * rows + half * count + jnp.where(lane >= count, lane - count, lane)
        for b in range(n):
            seen = pos_ref[b] * rows + row <= mine
            bias[b * rows : (b + 1) * rows, :] = jnp.where(seen, 0.0, NEGATIVE)

    def scores(first, scr):
        def part(h):
            return q_ref[h][:, half * count : (half + 1) * count]

        weights = jnp.concatenate([part(first + h) for h in range(4)], axis=1)
        piece = seq // PIECES
        for r in range(0, seq, piece):
            scr[r : r + piece, :] = jnp.dot(
                lat_ref[r : r + piece, :], weights, preferred_element_type=F32
            )
            yield

    def softmax(scr):
        scale = []
        for tile in (slice(0, lanes), slice(lanes, 2 * lanes)):
            top = None
            for r in range(0, seq, run):
                v = scr[r : r + run, tile] + bias[r : r + run, :]
                top = v if top is None else jnp.maximum(top, v)
                yield
            top = jnp.max(top, axis=0, keepdims=True)
            total = None
            for r in range(0, seq, run):
                v = scr[r : r + run, tile] + bias[r : r + run, :]
                p = jnp.exp2((v - top) * (SCALE_ATTN * LOG2E))
                scr[r : r + run, tile] = p
                total = p if total is None else total + p
                yield
            total = jnp.sum(total, axis=0, keepdims=True)
            scale.append(1.0 / (HEADS * total))
        for r in range(0, seq, run):
            acc[r : r + run, :] += (
                scr[r : r + run, :lanes] * scale[0] + scr[r : r + run, lanes:] * scale[1]
            )
            yield

    def together(dots, vectors):
        per = -(-5 * (seq // run) // PIECES)
        for _ in dots:
            for _ in range(per):
                next(vectors, None)
        for _ in vectors:
            pass

    together(scores(0, scr_a), softmax(scr_b))

    @pl.when(step == 0)
    def _():
        acc[...] = jnp.zeros_like(acc)

    together(scores(4, scr_b), softmax(scr_a))

    @pl.when(step == pl.num_programs(0) - 1)
    def _():
        for _ in softmax(scr_b):
            pass
        both = jnp.transpose(acc[...])
        out = both[:count] + both[count:]
        out_ref[...] = out
        low_ref[...] = out.astype(BF16)


def attend(q, lat, block_pos, mine, half, n):
    heads, depth, lanes = q.shape
    seq = lat.shape[0]
    count = lanes // 2
    smem = pl.BlockSpec(memory_space=pltpu.SMEM)
    whole = lambda i: (0, 0)
    return pl.pallas_call(
        functools.partial(attend_kernel, half, n),
        grid=(heads // 8,),
        out_shape=(
            jax.ShapeDtypeStruct((count, seq), F32),
            jax.ShapeDtypeStruct((count, seq), BF16),
        ),
        in_specs=[
            pl.BlockSpec((8, depth, lanes), lambda i: (i, 0, 0)),
            pl.BlockSpec((seq, depth), whole),
            smem,
            smem,
        ],
        out_specs=(pl.BlockSpec((count, seq), whole), pl.BlockSpec((count, seq), whole)),
        scratch_shapes=[
            pltpu.VMEM((seq, 2 * lanes), F32),
            pltpu.VMEM((seq, 2 * lanes), F32),
            pltpu.VMEM((seq, lanes), F32),
            pltpu.VMEM((seq, lanes), F32),
        ],
        compiler_params=pltpu.CompilerParams(vmem_limit_bytes=VMEM_LIMIT),
        cost_estimate=pl.CostEstimate(
            flops=count * heads * seq * depth // 8,
            bytes_accessed=4 * count * heads * depth,
            transcendentals=0,
        ),
        name="attend",
    )(q, lat, block_pos, mine)


def back_kernel(heads, last, iq_ref, w_ref, key_ref, post_ref, poss_ref, *rest):
    peers_i = rest[0]
    own_i, own_t, peers_t = rest[1:4]
    gq_ref, gk_ref, scr, coef, acc, dscr = rest[-6:]
    step = pl.program_id(0)

    @pl.when(step == 0)
    def _():
        acc[...] = rest[4][...] if last else jnp.zeros_like(acc)

    scr[...] = dot_t(iq_ref[...], key_ref[...])
    index, target = own_i[...], own_t[...]
    for k in range(peers_i.shape[0]):
        index = index + peers_i[k]
        target = target + peers_t[k].astype(F32)
    seen = poss_ref[...] <= post_ref[...]
    masked = jnp.where(seen, index, NEGATIVE)
    weights = jnp.where(seen, jnp.exp(masked - jnp.max(masked, axis=1, keepdims=True)), 0.0)
    prob = weights * (1.0 / jnp.sum(weights, axis=1, keepdims=True))
    dscr[...] = jnp.where(seen, LOSS_SCALE * (prob - target), 0.0).astype(BF16).astype(F32)
    for t in range(TOK):
        for g in range(0, heads, 8):
            r = t * heads + g
            value = dscr[t : t + 1, :] * w_ref[r : r + 8, 0:1]
            coef[r : r + 8, :] = jnp.where(scr[r : r + 8, :] > 0.0, value, 0.0).astype(BF16)
    gq_ref[...] = jnp.dot(coef[...], key_ref[...], preferred_element_type=F32)
    acc[...] += lax.dot_general(
        iq_ref[...], coef[...], (((0,), (0,)), ((), ())), preferred_element_type=F32
    )

    @pl.when(step == pl.num_programs(0) - 1)
    def _():
        if last:
            gk_ref[...] = jnp.transpose(acc[...]).astype(BF16)
        else:
            gk_ref[...] = acc[...]


def back(iq, wide, keys, pos_t, pos_s, peers_i, own_i, own_t, peers_t, carried, heads, first, last):
    depth = iq.shape[1]
    seq = keys.shape[0]
    count = own_t.shape[0]
    m = TOK * heads
    off = first // TOK
    others = peers_i.shape[0]
    return pl.pallas_call(
        functools.partial(back_kernel, heads, last),
        grid=(count // TOK,),
        out_shape=(
            jax.ShapeDtypeStruct(iq.shape, F32),
            jax.ShapeDtypeStruct((seq, depth), BF16)
            if last
            else jax.ShapeDtypeStruct((depth, seq), F32),
        ),
        in_specs=[
            pl.BlockSpec((m, depth), lambda i: (i + off, 0)),
            pl.BlockSpec((m, wide.shape[1]), lambda i: (i + off, 0)),
            pl.BlockSpec((seq, depth), lambda i: (0, 0)),
            pl.BlockSpec((TOK, 1), lambda i: (i + off, 0)),
            pl.BlockSpec((1, seq), lambda i: (0, 0)),
            pl.BlockSpec((others, TOK, seq), lambda i: (0, i + off, 0)),
            pl.BlockSpec((TOK, seq), lambda i: (i + off, 0)),
            pl.BlockSpec((TOK, seq), lambda i: (i, 0)),
            pl.BlockSpec((others, TOK, seq), lambda i: (0, i, 0)),
        ]
        + [pl.BlockSpec((depth, seq), lambda i: (0, 0)), pl.BlockSpec(memory_space=pl.ANY)] * last,
        input_output_aliases={10: 0} if last else {},
        out_specs=(
            pl.BlockSpec((m, depth), lambda i: (i + off, 0)),
            pl.BlockSpec((seq, depth) if last else (depth, seq), lambda i: (0, 0)),
        ),
        scratch_shapes=[
            pltpu.VMEM((m, seq), F32),
            pltpu.VMEM((m, seq), BF16),
            pltpu.VMEM((depth, seq), F32),
            pltpu.VMEM((TOK, seq), F32),
        ],
        compiler_params=pltpu.CompilerParams(vmem_limit_bytes=VMEM_LIMIT),
        cost_estimate=pl.CostEstimate(
            flops=8 * count * heads * seq * depth,
            bytes_accessed=8 * count * heads * depth,
            transcendentals=0,
        ),
        name="back",
    )(iq, wide, keys, pos_t, pos_s, peers_i, own_i, own_t, peers_t, *carried)


def scatter_kernel(
    n, ranks, gk_ref, out_ref, got1, sum1, put2, got2, sum2, put3, got3, put4, got4, ssem, rsem
):
    z, x, c, a = place(n)
    y = lax.axis_index("head")
    barrier = pltpu.get_barrier_semaphore()
    greeted = [dict(ctx=at(z, 1 - x, c)), dict(ctx=at(z, x, 1 - c))]
    greeted += [dict(ctx=at(lax.rem(z + d, a), x, c)) for d in range(1, a)]
    greeted += [dict(head=lax.rem(y + d, ranks)) for d in range(1, ranks)]
    for where in greeted:
        pl.semaphore_signal(barrier, inc=1, device_id=where, device_id_type=MESH)
    pl.semaphore_wait(barrier, len(greeted))

    first = remote(gk_ref.at[:, :, 1 - c], got1, ssem.at[0], rsem.at[0], ctx=at(z, x, 1 - c))
    first.start()
    first.wait()
    sum1[...] = gk_ref[:, :, c].astype(F32) + got1[...].astype(F32)
    put2[...] = sum1[:, 1 - x].astype(BF16)
    second = remote(put2, got2, ssem.at[1], rsem.at[1], ctx=at(z, 1 - x, c))
    second.start()
    second.wait()
    sum2[...] = sum1[:, x] + got2[...].astype(F32)
    put3[...] = sum2[...].astype(BF16)
    third = []
    for d in range(1, a):
        to = lax.rem(z + d, a)
        item = remote(
            put3.at[to], got3.at[d - 1], ssem.at[1 + d], rsem.at[1 + d], ctx=at(to, x, c)
        )
        item.start()
        third.append(item)
    for item in third:
        item.wait()
    part = sum2[z]
    for d in range(1, a):
        part = part + got3[d - 1].astype(F32)
    put4[...] = part
    fourth = []
    for d in range(1, ranks):
        item = remote(
            put4,
            got4.at[d - 1],
            ssem.at[a + d],
            rsem.at[a + d],
            head=lax.rem(y + d, ranks),
        )
        item.start()
        fourth.append(item)
    for item in fourth:
        item.wait()
    part = put4[...]
    for d in range(1, ranks):
        part = part + got4[d - 1]
    out_ref[...] = part


def scatter(gk, n, ranks):
    a = n // 4
    rows, depth = gk.shape[0] // n, gk.shape[1]
    vmem = pl.BlockSpec(memory_space=pltpu.VMEM)
    return pl.pallas_call(
        functools.partial(scatter_kernel, n, ranks),
        out_shape=jax.ShapeDtypeStruct((rows, depth), F32),
        in_specs=[vmem],
        out_specs=vmem,
        scratch_shapes=[
            pltpu.VMEM((a, 2, rows, depth), BF16),
            pltpu.VMEM((a, 2, rows, depth), F32),
            pltpu.VMEM((a, rows, depth), BF16),
            pltpu.VMEM((a, rows, depth), BF16),
            pltpu.VMEM((a, rows, depth), F32),
            pltpu.VMEM((a, rows, depth), BF16),
            pltpu.VMEM((a - 1, rows, depth), BF16),
            pltpu.VMEM((rows, depth), F32),
            pltpu.VMEM((ranks - 1, rows, depth), F32),
            pltpu.SemaphoreType.DMA((a + ranks,)),
            pltpu.SemaphoreType.DMA((a + ranks,)),
        ],
        compiler_params=pltpu.CompilerParams(collective_id=1, has_side_effects=True),
        name="scatter",
    )(gk.reshape(a, 2, 2, rows, depth))


def swap(value, ranks):
    return jnp.stack(
        [
            lax.ppermute(value, "head", [(i, (i + d) % ranks) for i in range(ranks)])
            for d in range(1, ranks)
        ]
    )


def body(queries, latents, index_queries, index_keys, head_weights, block_pos):
    rows, heads, rank = queries.shape
    depth = index_queries.shape[2]
    n, ranks = lax.axis_size("ctx"), lax.axis_size("head")
    seq = rows * n
    q = jnp.transpose(queries, (1, 2, 0))
    iq = index_queries.reshape(rows * heads, depth)
    wide = jnp.broadcast_to(
        (head_weights * depth ** (-0.5))[:, :, None], (rows, heads, 128)
    ).reshape(rows * heads, 128)
    local = jnp.arange(rows, dtype=jnp.int32)
    pos_s = (block_pos[:, None] * rows + local[None, :]).reshape(1, seq)
    mine = jnp.sum(jnp.where(jnp.arange(n) == lax.axis_index("ctx"), block_pos, 0))
    pos_t = (mine * rows + local)[:, None]

    lat, keys, own_i = gather(latents, index_keys, iq, wide, heads, n)
    lat = lat.reshape(seq, rank)
    keys = keys.reshape(seq, depth)
    peers_i = swap(own_i, ranks)
    own_t, peers_t = [], []
    for k in range(2):
        full, low = attend(q, lat, block_pos, mine[None], k, n)
        own_t.append(full)
        peers_t.append(swap(low, ranks))
    grads = ()
    for k in range(2):
        grad_queries, carry = back(
            iq, wide, keys, pos_t, pos_s, peers_i, own_i, own_t[k], peers_t[k], grads, heads,
            k * (rows // 2), k == 1,
        )
        grads = (carry, grad_queries)
    return grad_queries.reshape(rows, heads, depth), scatter(carry, n, ranks)


def solution(mesh):
    return jax.shard_map(
        body,
        mesh=mesh,
        in_specs=(
            P("ctx", "head", None),
            P("ctx", None),
            P("ctx", "head", None),
            P("ctx", None),
            P("ctx", "head"),
            P(),
        ),
        out_specs=(P("ctx", "head", None), P("ctx", None)),
        check_vma=False,
    )
```

```python
import functools
import math

import jax
import jax.numpy as jnp
from jax import lax
from jax.experimental import pallas as pl
from jax.experimental.pallas import tpu as pltpu
from jax.sharding import PartitionSpec as P

HEADS = 64
SCALE_ATTN = 192.0 ** (-0.5)
LOSS_SCALE = 1024.0
NEGATIVE = -1e30
LOG2E = math.log2(math.e)
MESH = pl.DeviceIdType.MESH
F32 = jnp.float32
BF16 = jnp.bfloat16
TOK = 8
ITOK = 8
PIECES = 8
VMEM_LIMIT = 60 * 1024 * 1024


def place(n):
    me = lax.axis_index("ctx")
    a = n // 4
    return me // 4, (me // 2) % 2, me % 2, a


def at(z, x, c):
    return (z * 2 + x) * 2 + c


def remote(src, dst, send, recv, **where):
    return pltpu.make_async_remote_copy(
        src_ref=src, dst_ref=dst, send_sem=send, recv_sem=recv, device_id=where, device_id_type=MESH
    )


def dot_t(a, b):
    return lax.dot_general(a, b, (((1,), (1,)), ((), ())), preferred_element_type=F32)


def gather_kernel(
    n, heads, lat_ref, key_ref, iq_ref, w_ref, lat_out, key_out, idx_ref,
    scr_a, scr_b, send_sem, recv_sem, own_sem,
):
    z, x, c, a = place(n)
    y = lax.axis_index("head")
    other_y = y + 1 - 2 * (y % 2)
    partner = at(z, x, 1 - c)
    barrier = pltpu.get_barrier_semaphore()

    def greet(**where):
        pl.semaphore_signal(barrier, inc=1, device_id=where, device_id_type=MESH)

    greet(ctx=at(z, 1 - x, c))
    greet(ctx=partner)
    greet(head=other_y)

    for d in range(1, a):
        greet(ctx=at((z + d) % a, x, c))

    me = at(z, x, c)
    owns = []
    for k, (src, dst) in enumerate(((key_ref, key_out), (lat_ref, lat_out))):
        own = pltpu.make_async_copy(src, dst.at[me], own_sem.at[k])
        own.start()
        owns.append(own)
    pl.semaphore_wait(barrier, 2 + a)

    rows = lat_ref.shape[0]
    part = rows // 2

    def piece(ref, k):
        return ref.at[pl.ds(pl.multiple_of((k - 1) * part, part), part)]

    def copy(k, slot, way, first, **where):
        if isinstance(k, int) and k == 0:
            src, dst = (key_ref if first else key_out.at[slot]), key_out.at[slot]
        else:
            dst = piece(lat_out.at[slot], k)
            src = piece(lat_ref, k) if first else dst
        return remote(src, dst, send_sem.at[k, slot, way], recv_sem.at[k, slot], **where)

    def to_core(k, slot, first=False):
        return copy(k, slot, 0, first, ctx=partner)

    def to_x(k, slot, first=False):
        return copy(k, slot, 1, first, ctx=at(z, 1 - x, c))

    def to_y(k, slot):
        return copy(k, slot, 2, False, head=other_y)

    def arrived(k, slot):
        to_core(k, slot).wait_recv()

    def line(k, slot, act):
        for d in range(1, a):
            act(copy(k, slot, 4 + d, True, ctx=at((z + d) % a, x, c)))

    def sides(d, act):
        for side in (1, -1) if d > 0 else (0,):
            zs = z - d if side >= 0 else z + d
            if d == 0:
                act(zs, side)
            else:
                ok = zs >= 0 if side > 0 else zs < a
                pl.when(ok)(functools.partial(act, zs, side))

    start = lambda item: item.start()
    done = lambda item: item.wait_send()
    mine, others = 1 + y % 2, 2 - y % 2

    def column(ks, d, wait, act):
        def go(zs, side):
            slot = at(zs, x, c)
            for k in ks:
                if wait and d > 0:
                    arrived(k, slot)
                if d == 0:
                    line(k, slot, act)
            crossing = 0 if ks == (0,) else mine
            act(to_x(crossing, slot, d == 0))
            for k in ks:
                act(to_core(k, slot, d == 0))

        sides(d, go)

    def crossed(k, d, wait, act, onward):
        def go(zs, side):
            slot = at(zs, 1 - x, c)
            if wait:
                arrived(k, slot)
            if onward:
                act(to_y(k, slot))
            act(to_core(k, slot))

        sides(d, go)

    column((0,), 0, True, start)
    for d in range(1, a):
        column((0,), d, True, start)
    column((1, 2), 0, True, start)
    for d in range(a):
        crossed(0, d, True, start, False)

    owns[0].wait()
    for zs in range(a):
        for xs in range(2):
            arrived(0, at(zs, xs, 1 - c))

    stages = []
    for d in range(a + 2):
        if 1 <= d < a:
            stages.append(functools.partial(column, (1, 2), d, True, start))
        if 1 <= d <= a:
            stages.append(functools.partial(crossed, mine, d - 1, True, start, True))
        if 2 <= d:
            stages.append(functools.partial(crossed, others, d - 2, True, start, False))

    depth = iq_ref.shape[1]
    m = ITOK * heads
    width = 4 * rows

    def index_chunk(i, _):
        iq = iq_ref[pl.ds(pl.multiple_of(i * m, m), m), :]
        w = w_ref.at[pl.ds(pl.multiple_of(i * m, m), m)]
        out = idx_ref.at[pl.ds(pl.multiple_of(i * ITOK, ITOK), ITOK)]
        scrs = (scr_a, scr_b)

        def reduce(p):
            scr = scrs[p % 2]
            sums = []
            for t in range(ITOK):
                acc = None
                for g in range(0, heads, 8):
                    r = t * heads + g
                    term = jnp.maximum(scr[r : r + 8, :], 0.0) * jnp.concatenate(
                        [w[r : r + 8, :]] * (width // 128), axis=1
                    )
                    acc = term if acc is None else acc + term
                sums.append(jnp.sum(acc, axis=0, keepdims=True))
            out[:, p * width : (p + 1) * width] = jnp.concatenate(sums, axis=0)

        count = n * rows // width
        per = width // rows
        for p in range(count):
            held = key_out[p * per : (p + 1) * per].reshape(width, depth)
            scrs[p % 2][...] = dot_t(iq, held)
            if p > 0:
                reduce(p - 1)
        reduce(count - 1)
        return 0

    chunks = iq_ref.shape[0] // m
    lead = chunks // 4
    count = len(stages)
    cut = [0] + [lead + (chunks - lead) * d // count for d in range(count)] + [chunks]
    for d in range(count + 1):
        if cut[d + 1] > cut[d]:
            lax.fori_loop(cut[d], cut[d + 1], index_chunk, 0)
        if d < count:
            stages[d]()

    owns[1].wait()
    for zs in range(a):
        for xs in range(2):
            for k in (1, 2):
                arrived(k, at(zs, xs, 1 - c))
    for ks in ((0,), (1, 2)):
        for d in range(a):
            column(ks, d, False, done)
    for d in range(a):
        crossed(0, d, False, done, False)
        crossed(mine, d, False, done, True)
        crossed(others, d, False, done, False)


def gather(latents, keys, iq, wide, heads, n):
    rows = latents.shape[0]
    seq = rows * n
    hbm = pl.BlockSpec(memory_space=pl.ANY)
    vmem = pl.BlockSpec(memory_space=pltpu.VMEM)
    m = ITOK * heads
    return pl.pallas_call(
        functools.partial(gather_kernel, n, heads),
        out_shape=(
            jax.ShapeDtypeStruct((n, rows, latents.shape[1]), BF16),
            jax.ShapeDtypeStruct((n, rows, keys.shape[1]), BF16),
            jax.ShapeDtypeStruct((iq.shape[0] // heads, seq), F32),
        ),
        in_specs=[hbm, hbm, vmem, vmem],
        out_specs=(hbm, vmem, vmem),
        scratch_shapes=[
            pltpu.VMEM((m, 4 * rows), F32),
            pltpu.VMEM((m, 4 * rows), F32),
            pltpu.SemaphoreType.DMA((3, n, 4 + n // 4)),
            pltpu.SemaphoreType.DMA((3, n)),
            pltpu.SemaphoreType.DMA((2,)),
        ],
        compiler_params=pltpu.CompilerParams(
            collective_id=0, has_side_effects=True, vmem_limit_bytes=VMEM_LIMIT
        ),
        name="gather",
    )(latents, keys, iq, wide)


def attend_kernel(
    half, n, q_ref, lat_ref, pos_ref, mine_ref, out_ref, low_ref, scr_a, scr_b, bias, acc
):
    step = pl.program_id(0)
    seq = lat_ref.shape[0]
    lanes = q_ref.shape[2]
    count = lanes // 2
    rows = seq // n
    run = 64

    @pl.when(step == 0)
    def _():
        lane = lax.broadcasted_iota(jnp.int32, (rows, lanes), 1)
        row = lax.broadcasted_iota(jnp.int32, (rows, lanes), 0)
        mine = mine_ref[0] * rows + half * count + jnp.where(lane >= count, lane - count, lane)
        for b in range(n):
            seen = pos_ref[b] * rows + row <= mine
            bias[b * rows : (b + 1) * rows, :] = jnp.where(seen, 0.0, NEGATIVE)

    def scores(first, scr):
        def part(h):
            return q_ref[h][:, half * count : (half + 1) * count]

        weights = jnp.concatenate([part(first + h) for h in range(4)], axis=1)
        piece = seq // PIECES
        for r in range(0, seq, piece):
            scr[r : r + piece, :] = jnp.dot(
                lat_ref[r : r + piece, :], weights, preferred_element_type=F32
            )
            yield

    def softmax(scr):
        scale = []
        for tile in (slice(0, lanes), slice(lanes, 2 * lanes)):
            top = None
            for r in range(0, seq, run):
                v = scr[r : r + run, tile] + bias[r : r + run, :]
                top = v if top is None else jnp.maximum(top, v)
                yield
            top = jnp.max(top, axis=0, keepdims=True)
            total = None
            for r in range(0, seq, run):
                v = scr[r : r + run, tile] + bias[r : r + run, :]
                p = jnp.exp2((v - top) * (SCALE_ATTN * LOG2E))
                scr[r : r + run, tile] = p
                total = p if total is None else total + p
                yield
            total = jnp.sum(total, axis=0, keepdims=True)
            scale.append(1.0 / (HEADS * total))
        for r in range(0, seq, run):
            acc[r : r + run, :] += (
                scr[r : r + run, :lanes] * scale[0] + scr[r : r + run, lanes:] * scale[1]
            )
            yield

    def together(dots, vectors):
        per = -(-5 * (seq // run) // PIECES)
        for _ in dots:
            for _ in range(per):
                next(vectors, None)
        for _ in vectors:
            pass

    together(scores(0, scr_a), softmax(scr_b))

    @pl.when(step == 0)
    def _():
        acc[...] = jnp.zeros_like(acc)

    together(scores(4, scr_b), softmax(scr_a))

    @pl.when(step == pl.num_programs(0) - 1)
    def _():
        for _ in softmax(scr_b):
            pass
        both = jnp.transpose(acc[...])
        out = both[:count] + both[count:]
        out_ref[...] = out
        low_ref[...] = out.astype(BF16)


def attend(q, lat, block_pos, mine, half, n):
    heads, depth, lanes = q.shape
    seq = lat.shape[0]
    count = lanes // 2
    smem = pl.BlockSpec(memory_space=pltpu.SMEM)
    whole = lambda i: (0, 0)
    return pl.pallas_call(
        functools.partial(attend_kernel, half, n),
        grid=(heads // 8,),
        out_shape=(
            jax.ShapeDtypeStruct((count, seq), F32),
            jax.ShapeDtypeStruct((count, seq), BF16),
        ),
        in_specs=[
            pl.BlockSpec((8, depth, lanes), lambda i: (i, 0, 0)),
            pl.BlockSpec((seq, depth), whole),
            smem,
            smem,
        ],
        out_specs=(pl.BlockSpec((count, seq), whole), pl.BlockSpec((count, seq), whole)),
        scratch_shapes=[
            pltpu.VMEM((seq, 2 * lanes), F32),
            pltpu.VMEM((seq, 2 * lanes), F32),
            pltpu.VMEM((seq, lanes), F32),
            pltpu.VMEM((seq, lanes), F32),
        ],
        compiler_params=pltpu.CompilerParams(vmem_limit_bytes=VMEM_LIMIT),
        cost_estimate=pl.CostEstimate(
            flops=count * heads * seq * depth // 8,
            bytes_accessed=4 * count * heads * depth,
            transcendentals=0,
        ),
        name="attend",
    )(q, lat, block_pos, mine)


def back_kernel(heads, last, iq_ref, w_ref, key_ref, post_ref, poss_ref, *rest):
    peers_i = rest[0]
    own_i, own_t, peers_t = rest[1:4]
    gq_ref, gk_ref, scr, coef, acc, dscr = rest[-6:]
    step = pl.program_id(0)

    @pl.when(step == 0)
    def _():
        acc[...] = rest[4][...] if last else jnp.zeros_like(acc)

    scr[...] = dot_t(iq_ref[...], key_ref[...])
    index, target = own_i[...], own_t[...]
    for k in range(peers_i.shape[0]):
        index = index + peers_i[k]
        target = target + peers_t[k].astype(F32)
    seen = poss_ref[...] <= post_ref[...]
    masked = jnp.where(seen, index, NEGATIVE)
    weights = jnp.where(seen, jnp.exp(masked - jnp.max(masked, axis=1, keepdims=True)), 0.0)
    prob = weights * (1.0 / jnp.sum(weights, axis=1, keepdims=True))
    dscr[...] = jnp.where(seen, LOSS_SCALE * (prob - target), 0.0).astype(BF16).astype(F32)
    for t in range(TOK):
        for g in range(0, heads, 8):
            r = t * heads + g
            wide = jnp.concatenate([w_ref[r : r + 8, :]] * (dscr.shape[1] // 128), axis=1)
            value = dscr[t : t + 1, :] * wide
            coef[r : r + 8, :] = jnp.where(scr[r : r + 8, :] > 0.0, value, 0.0).astype(BF16)
    gq_ref[...] = jnp.dot(coef[...], key_ref[...], preferred_element_type=F32)
    acc[...] += lax.dot_general(
        iq_ref[...], coef[...], (((0,), (0,)), ((), ())), preferred_element_type=F32
    )

    @pl.when(step == pl.num_programs(0) - 1)
    def _():
        if last:
            gk_ref[...] = jnp.transpose(acc[...]).astype(BF16)
        else:
            gk_ref[...] = acc[...]


def back(iq, wide, keys, pos_t, pos_s, peers_i, own_i, own_t, peers_t, carried, heads, first, last):
    depth = iq.shape[1]
    seq = keys.shape[0]
    count = own_t.shape[0]
    m = TOK * heads
    off = first // TOK
    others = peers_i.shape[0]
    return pl.pallas_call(
        functools.partial(back_kernel, heads, last),
        grid=(count // TOK,),
        out_shape=(
            jax.ShapeDtypeStruct(iq.shape, F32),
            jax.ShapeDtypeStruct((seq, depth), BF16)
            if last
            else jax.ShapeDtypeStruct((depth, seq), F32),
        ),
        in_specs=[
            pl.BlockSpec((m, depth), lambda i: (i + off, 0)),
            pl.BlockSpec((m, wide.shape[1]), lambda i: (i + off, 0)),
            pl.BlockSpec((seq, depth), lambda i: (0, 0)),
            pl.BlockSpec((TOK, 1), lambda i: (i + off, 0)),
            pl.BlockSpec((1, seq), lambda i: (0, 0)),
            pl.BlockSpec((others, TOK, seq), lambda i: (0, i + off, 0)),
            pl.BlockSpec((TOK, seq), lambda i: (i + off, 0)),
            pl.BlockSpec((TOK, seq), lambda i: (i, 0)),
            pl.BlockSpec((others, TOK, seq), lambda i: (0, i, 0)),
        ]
        + [pl.BlockSpec((depth, seq), lambda i: (0, 0)), pl.BlockSpec(memory_space=pl.ANY)] * last,
        input_output_aliases={10: 0} if last else {},
        out_specs=(
            pl.BlockSpec((m, depth), lambda i: (i + off, 0)),
            pl.BlockSpec((seq, depth) if last else (depth, seq), lambda i: (0, 0)),
        ),
        scratch_shapes=[
            pltpu.VMEM((m, seq), F32),
            pltpu.VMEM((m, seq), BF16),
            pltpu.VMEM((depth, seq), F32),
            pltpu.VMEM((TOK, seq), F32),
        ],
        compiler_params=pltpu.CompilerParams(vmem_limit_bytes=VMEM_LIMIT),
        cost_estimate=pl.CostEstimate(
            flops=8 * count * heads * seq * depth,
            bytes_accessed=8 * count * heads * depth,
            transcendentals=0,
        ),
        name="back",
    )(iq, wide, keys, pos_t, pos_s, peers_i, own_i, own_t, peers_t, *carried)


def scatter_kernel(
    n, ranks, gk_ref, out_ref, got1, sum1, put2, got2, sum2, put3, got3, put4, got4, ssem, rsem
):
    z, x, c, a = place(n)
    y = lax.axis_index("head")
    barrier = pltpu.get_barrier_semaphore()
    greeted = [dict(ctx=at(z, 1 - x, c)), dict(ctx=at(z, x, 1 - c))]
    greeted += [dict(ctx=at(lax.rem(z + d, a), x, c)) for d in range(1, a)]
    greeted += [dict(head=lax.rem(y + d, ranks)) for d in range(1, ranks)]
    for where in greeted:
        pl.semaphore_signal(barrier, inc=1, device_id=where, device_id_type=MESH)
    pl.semaphore_wait(barrier, len(greeted))

    first = remote(gk_ref.at[:, :, 1 - c], got1, ssem.at[0], rsem.at[0], ctx=at(z, x, 1 - c))
    first.start()
    first.wait()
    sum1[...] = gk_ref[:, :, c].astype(F32) + got1[...].astype(F32)
    put2[...] = sum1[:, 1 - x].astype(BF16)
    second = remote(put2, got2, ssem.at[1], rsem.at[1], ctx=at(z, 1 - x, c))
    second.start()
    second.wait()
    sum2[...] = sum1[:, x] + got2[...].astype(F32)
    put3[...] = sum2[...].astype(BF16)
    third = []
    for d in range(1, a):
        to = lax.rem(z + d, a)
        item = remote(
            put3.at[to], got3.at[d - 1], ssem.at[1 + d], rsem.at[1 + d], ctx=at(to, x, c)
        )
        item.start()
        third.append(item)
    for item in third:
        item.wait()
    part = sum2[z]
    for d in range(1, a):
        part = part + got3[d - 1].astype(F32)
    put4[...] = part
    fourth = []
    for d in range(1, ranks):
        item = remote(
            put4,
            got4.at[d - 1],
            ssem.at[a + d],
            rsem.at[a + d],
            head=lax.rem(y + d, ranks),
        )
        item.start()
        fourth.append(item)
    for item in fourth:
        item.wait()
    part = put4[...]
    for d in range(1, ranks):
        part = part + got4[d - 1]
    out_ref[...] = part


def scatter(gk, n, ranks):
    a = n // 4
    rows, depth = gk.shape[0] // n, gk.shape[1]
    vmem = pl.BlockSpec(memory_space=pltpu.VMEM)
    return pl.pallas_call(
        functools.partial(scatter_kernel, n, ranks),
        out_shape=jax.ShapeDtypeStruct((rows, depth), F32),
        in_specs=[vmem],
        out_specs=vmem,
        scratch_shapes=[
            pltpu.VMEM((a, 2, rows, depth), BF16),
            pltpu.VMEM((a, 2, rows, depth), F32),
            pltpu.VMEM((a, rows, depth), BF16),
            pltpu.VMEM((a, rows, depth), BF16),
            pltpu.VMEM((a, rows, depth), F32),
            pltpu.VMEM((a, rows, depth), BF16),
            pltpu.VMEM((a - 1, rows, depth), BF16),
            pltpu.VMEM((rows, depth), F32),
            pltpu.VMEM((ranks - 1, rows, depth), F32),
            pltpu.SemaphoreType.DMA((a + ranks,)),
            pltpu.SemaphoreType.DMA((a + ranks,)),
        ],
        compiler_params=pltpu.CompilerParams(collective_id=1, has_side_effects=True),
        name="scatter",
    )(gk.reshape(a, 2, 2, rows, depth))


def swap(value, ranks):
    return jnp.stack(
        [
            lax.ppermute(value, "head", [(i, (i + d) % ranks) for i in range(ranks)])
            for d in range(1, ranks)
        ]
    )


def body(queries, latents, index_queries, index_keys, head_weights, block_pos):
    rows, heads, rank = queries.shape
    depth = index_queries.shape[2]
    n, ranks = lax.axis_size("ctx"), lax.axis_size("head")
    seq = rows * n
    q = jnp.transpose(queries, (1, 2, 0))
    iq = index_queries.reshape(rows * heads, depth)
    wide = jnp.broadcast_to(
        (head_weights * depth ** (-0.5))[:, :, None], (rows, heads, 128)
    ).reshape(rows * heads, 128)
    local = jnp.arange(rows, dtype=jnp.int32)
    pos_s = (block_pos[:, None] * rows + local[None, :]).reshape(1, seq)
    mine = jnp.sum(jnp.where(jnp.arange(n) == lax.axis_index("ctx"), block_pos, 0))
    pos_t = (mine * rows + local)[:, None]

    lat, keys, own_i = gather(latents, index_keys, iq, wide, heads, n)
    lat = lat.reshape(seq, rank)
    keys = keys.reshape(seq, depth)
    peers_i = swap(own_i, ranks)
    own_t, peers_t = [], []
    for k in range(2):
        full, low = attend(q, lat, block_pos, mine[None], k, n)
        own_t.append(full)
        peers_t.append(swap(low, ranks))
    grads = ()
    for k in range(2):
        grad_queries, carry = back(
            iq, wide, keys, pos_t, pos_s, peers_i, own_i, own_t[k], peers_t[k], grads, heads,
            k * (rows // 2), k == 1,
        )
        grads = (carry, grad_queries)
    return grad_queries.reshape(rows, heads, depth), scatter(carry, n, ranks)


def solution(mesh):
    return jax.shard_map(
        body,
        mesh=mesh,
        in_specs=(
            P("ctx", "head", None),
            P("ctx", None),
            P("ctx", "head", None),
            P("ctx", None),
            P("ctx", "head"),
            P(),
        ),
        out_specs=(P("ctx", "head", None), P("ctx", None)),
        check_vma=False,
    )
```
